32 devices in a mesh: parts: 2 (over y), ha: 4 (over x, core), wa: 4 (over z).
Axes of the slice: x: 2, y: 2, z: 4, core: 2. Of those that a mesh axis runs over, the one named last changes fastest.
Arguments:
- token_ids: int32 [64, 64], P(('parts', 'ha', 'wa')), parts along dimension 0, may hold values from 0 to 63999
- neighbour_lists: int32 [8, 8, 6], P(('parts', 'ha'), 'wa'), parts along dimension 0, may hold values from 0 to 8, as said below
- codebook: bfloat16 [39, 512], replicated, may hold values from -10 to 10
- qkv_weight: bfloat16 [2, 512, 1536], replicated, may hold values from -0.25 to 0.25
- out_weight: bfloat16 [2, 512, 512], replicated, may hold values from -0.25 to 0.25
- logit_scale: float32 [2, 8], replicated, may hold values from 1 to 32
- conv_weight: bfloat16 [3, 3, 512, 256], replicated, may hold values from -0.09375 to 0.09375
Outputs:
- decoded: bfloat16 [64, 64, 256], P(('parts', 'ha'), 'wa'), parts along dimension 0
The draws below stay inside these ranges and needn't reach their ends.
There are 2 independent parts, one for each index of `parts`. The reference program is written for one: setup_inputs(seed, part) draws one part's arguments, and reference() takes and returns one part's arrays. A program takes and returns all parts, laid end to end along the dimension named above; an argument that names none is the same for every part. Nothing has to cross between parts.
Inputs may be any that keep to these rules, and one draw needn't show every extreme that they name: `neighbour_lists`: each list holds 6 distinct neighbour numbers; the first is always 4, the block itself.
All inputs are finite; a program needn't handle non-finite values.
Results may differ from the reference program's by a relative error of at most 0.017.
Values may be sent and summed in bfloat16 or wider, within the bound.
No kernel may reach another device: no remote copies, remote signals or barrier semaphores. Data moves between devices by JAX's collectives and lax.ppermute only.
A program may use at most 64 MiB of HBM per device.

```python
import math
import jax
import jax.numpy as jnp
from jax import lax

D = 512
HEADS = 8
COUT = 256
VOCAB = 64000
LEVELS_SUM = 39
TILE = 8
NSEL = 6
BLOCKS = 2
H = 32
W = 64


def draw_neighbour_lists(key, part):
    count = H // TILE * (W // TILE)
    sub_key = jax.random.fold_in(key, 7)
    ranking = jax.random.randint(sub_key, (count, 8), 0, 1 << 20) * 8 + jnp.arange(8, dtype=jnp.int32)[None, :]
    order = jnp.argsort(ranking, axis=1)
    others = jnp.array([0, 1, 2, 3, 5, 6, 7, 8], jnp.int32)
    picked = jnp.take(others, order[:, :NSEL - 1])
    lists = jnp.concatenate([jnp.full((count, 1), 4, jnp.int32), picked.astype(jnp.int32)], axis=1)
    return lists.reshape(H // TILE, W // TILE, NSEL).astype(jnp.int32)


def draw_codebook(key, part):
    first, second = jax.random.split(jax.random.fold_in(key, 11), 2)
    scales = jnp.exp(jax.random.uniform(first, (LEVELS_SUM, 1), jnp.float32, math.log(0.5), math.log(5.0)))
    base = jnp.clip(jax.random.normal(second, (LEVELS_SUM, D), jnp.float32), -4.0, 4.0)
    return (base * scales / math.sqrt(6.0)).astype(jnp.bfloat16)


def draw_logit_scale(key, part):
    sub_key = jax.random.fold_in(key, 13)
    exponent = jax.random.uniform(sub_key, (BLOCKS, HEADS), jnp.float32, 0.0, math.log(4.0))
    return jnp.exp(exponent).astype(jnp.float32)


def with_ends(drawn, own_key, least, largest):
    longest = drawn.shape.index(max(drawn.shape))
    spots = []
    for shift in (0, 1):
        where = [jax.random.randint(jax.random.fold_in(own_key, axis), (), 0, length) for axis, length in enumerate(drawn.shape)]
        where[longest] = (where[longest] + shift) % drawn.shape[longest]
        spots.append(tuple(where))
    return drawn.at[spots[0]].set(least).at[spots[1]].set(largest)


def gaussian(key, shape, width, reach, held_as=jnp.bfloat16):
    entries = width * jax.random.normal(key, shape, jnp.float32)
    return jnp.clip(entries, min=-reach, max=reach).astype(held_as)


def setup_inputs(seed: int = 0, part: int = 0) -> dict:
    seeds = jax.random.split(jax.random.key(seed), 8)
    part_splits = jax.random.split(jax.random.fold_in(seeds[7], part), 8)
    token_ids = with_ends(jax.random.randint(part_splits[0], (H, W), 0, VOCAB), jax.random.fold_in(part_splits[0], 1), 0, VOCAB - 1).astype(jnp.int32)
    neighbour_lists = draw_neighbour_lists(jax.random.fold_in(jax.random.fold_in(seeds[7], part), 71), part)
    codebook = draw_codebook(jax.random.fold_in(seeds[7], 71), part)
    qkv_weight = gaussian(seeds[3], (BLOCKS, D, 3 * D), D ** -0.5, 0.25)
    out_weight = gaussian(seeds[4], (BLOCKS, D, D), D ** -0.5, 0.25)
    logit_scale = draw_logit_scale(jax.random.fold_in(seeds[7], 71), part)
    conv_weight = gaussian(seeds[6], (3, 3, D, COUT), (9 * D) ** -0.5, 0.09375)
    return {"token_ids": token_ids, "neighbour_lists": neighbour_lists, "codebook": codebook, "qkv_weight": qkv_weight, "out_weight": out_weight, "logit_scale": logit_scale, "conv_weight": conv_weight}


digit_levels = (8, 8, 8, 5, 5, 5)
norm_eps = 1e-06

def digit_slots(token_ids):
    result = []
    stride = 1
    for position in range(len(digit_levels) - 1, -1, -1):
        level_size = digit_levels[position]
        offset = sum(digit_levels[:position])
        result.append(offset + token_ids // stride % level_size)
        stride = stride * level_size
    return result

def normalize(values):
    wide32 = values.astype(jnp.float32)
    return wide32 * lax.rsqrt(lax.optimization_barrier(jnp.mean(wide32 * wide32, axis=-1, keepdims=True)) + norm_eps)

def head_norm(values):
    shaped = values.reshape(values.shape[:-1] + (HEADS, D // HEADS))
    return normalize(shaped).reshape(values.shape).astype(jnp.bfloat16)

def reference(token_ids, neighbour_lists, codebook, qkv_weight, out_weight, logit_scale, conv_weight):
    head_size = D // HEADS
    tile_rows = H // TILE
    tile_cols = W // TILE
    area = TILE * TILE
    running = jnp.zeros((H, W, D), jnp.float32)
    for table_row in digit_slots(token_ids):
        running = running + codebook[table_row].astype(jnp.float32)
    hidden = running.astype(jnp.bfloat16)
    row_pos = jnp.arange(H + 2 * TILE, dtype=jnp.int32) - TILE
    col_pos = jnp.arange(W + 2 * TILE, dtype=jnp.int32) - TILE
    inside = ((row_pos >= 0) & (row_pos < H))[:, None] & ((col_pos >= 0) & (col_pos < W))[None, :]
    key_valid = inside.reshape(tile_rows + 2, TILE, tile_cols + 2, TILE).transpose(0, 2, 1, 3).reshape(tile_rows + 2, tile_cols + 2, area)
    for layer_index in range(BLOCKS):
        normed = normalize(hidden).astype(jnp.bfloat16)
        combined = jnp.dot(normed, qkv_weight[layer_index], preferred_element_type=jnp.float32)
        queries = head_norm(combined[..., :D])
        keys = head_norm(combined[..., D:2 * D])
        values = combined[..., 2 * D:].astype(jnp.bfloat16)
        pair = jnp.concatenate([keys, values], axis=-1)
        padded = jnp.pad(pair, ((TILE, TILE), (TILE, TILE), (0, 0)))
        key_tiles = padded.reshape(tile_rows + 2, TILE, tile_cols + 2, TILE, 2 * D).transpose(0, 2, 1, 3, 4).reshape(tile_rows + 2, tile_cols + 2, area, 2 * D)
        query_tiles = queries.reshape(tile_rows, TILE, tile_cols, TILE, D).transpose(0, 2, 1, 3, 4).reshape(tile_rows, tile_cols, area, D)
        factor = logit_scale[layer_index].astype(jnp.float32) / math.sqrt(head_size)

        def tile_row(row_index):
            lists = neighbour_lists[row_index]
            row_sel = row_index + lists // 3
            col_sel = jnp.arange(tile_cols, dtype=jnp.int32)[:, None] + lists % 3
            gathered = key_tiles[row_sel, col_sel].reshape(tile_cols, NSEL * area, 2, HEADS, head_size)
            allowed = key_valid[row_sel, col_sel].reshape(tile_cols, NSEL * area)
            key_part = gathered[:, :, 0].astype(jnp.float32)
            value_part = gathered[:, :, 1].astype(jnp.float32)
            query_part = query_tiles[row_index].reshape(tile_cols, area, HEADS, head_size).astype(jnp.float32)
            scores = jnp.einsum('tqhd,tkhd->thqk', query_part, key_part) * factor[None, :, None, None]
            scores = jnp.where(allowed[:, None, None, :], scores, -1e+30)
            peak = lax.optimization_barrier(jnp.max(scores, axis=-1, keepdims=True))
            expo = jnp.exp(scores - peak)
            soft = (expo / lax.optimization_barrier(jnp.sum(expo, axis=-1, keepdims=True))).astype(jnp.bfloat16)
            mixed = jnp.einsum('thqk,tkhd->tqhd', soft.astype(jnp.float32), value_part)
            return mixed.reshape(tile_cols, area, D).astype(jnp.bfloat16)
        attended = lax.map(tile_row, jnp.arange(tile_rows, dtype=jnp.int32))
        attended = attended.reshape(tile_rows, tile_cols, TILE, TILE, D).transpose(0, 2, 1, 3, 4).reshape(H, W, D)
        hidden = (hidden.astype(jnp.float32) + jnp.dot(attended, out_weight[layer_index], preferred_element_type=jnp.float32)).astype(jnp.bfloat16)
    activated = jax.nn.silu(normalize(hidden)).astype(jnp.bfloat16)
    padded = jnp.pad(activated, ((1, 1), (1, 1), (0, 0)))
    running = jnp.zeros((H, W, COUT), jnp.float32)
    for shift_row in range(3):
        for shift_col in range(3):
            running = running + jnp.dot(padded[shift_row:shift_row + H, shift_col:shift_col + W], conv_weight[shift_row, shift_col], preferred_element_type=jnp.float32)
    return running.astype(jnp.bfloat16)
```

```python
import functools
import math

import jax
import jax.numpy as jnp
from jax import lax
from jax.experimental import pallas as pl
from jax.experimental.pallas import tpu as pltpu
from jax.sharding import PartitionSpec as P

D = 512
HEADS = 8
HEAD = D // HEADS
TILE = 8
AREA = TILE * TILE
NSEL = 6
BLOCKS = 2
HALF = 256
GROUP = HALF // HEAD
digit_levels = (8, 8, 8, 5, 5, 5)
digit_shift = (6, 3, 0, 9, 12, 15)
norm_eps = 1e-06
LOG2E = math.log2(math.e)
NEG = -1e30

f32 = jnp.float32
bf16 = jnp.bfloat16
i32 = jnp.int32


def mm(a, b):
    return lax.dot_general(a, b, (((1,), (0,)), ((), ())), preferred_element_type=f32)


def mm_t(a, b):
    return lax.dot_general(a, b, (((1,), (1,)), ((), ())), preferred_element_type=f32)


def tiles_at_once(count):
    return max(n for n in range(1, 5) if count % n == 0)


def pack_digits(ids):
    x = ids.astype(f32)
    q5 = jnp.floor((x + 0.5) * 0.2)
    q4 = jnp.floor((q5 + 0.5) * 0.2)
    q3 = jnp.floor((q4 + 0.5) * 0.2)
    return q3 + 512.0 * (q4 - 5.0 * q3) + 4096.0 * (q5 - 5.0 * q4) + 32768.0 * (x - 5.0 * q5)


def slot_tables():
    lane = lax.broadcasted_iota(i32, (1, 128), 1)
    slot = lane & 63
    shift = jnp.zeros_like(lane)
    start = jnp.zeros_like(lane)
    offset = 0
    for size, bits in zip(digit_levels, digit_shift):
        here = slot >= offset
        shift = jnp.where(here, bits, shift)
        start = jnp.where(here, offset, start)
        offset += size
    return shift, jnp.where(slot < offset, slot - start, -1)


def head_scale(x, ones_bd, floor):
    parts = []
    for half in range(D // HALF):
        piece = x[:, HALF * half : HALF * half + HALF]
        total = mm((piece * piece).astype(bf16), ones_bd)
        parts.append((piece * lax.rsqrt(total * (1.0 / HEAD) + floor)).astype(bf16))
    return jnp.concatenate(parts, axis=1)


def square_mean(x):
    return jnp.sum(x * x, axis=-1, keepdims=True) * (1.0 / D)


def attend_tile(q, starts, bias, factors, keys, values, lane_head):
    outs = []
    for g in range(D // HALF):
        cols = slice(HALF * g, HALF * g + HALF)
        qg = q[:, cols]
        q_bd = jnp.concatenate(
            [jnp.where(lane_head == h, qg, jnp.zeros_like(qg)) for h in range(GROUP)], axis=0
        )
        k = jnp.concatenate([keys[pl.ds(s, AREA), cols] for s in starts], axis=0)
        v = jnp.concatenate([values[pl.ds(s, AREA), cols] for s in starts], axis=0)
        s = mm_t(q_bd, k) + bias
        s = s - jnp.max(s, axis=-1, keepdims=True)
        p = jnp.concatenate(
            [
                jnp.exp2(s[AREA * h : AREA * h + AREA] * factors[GROUP * g + h])
                for h in range(GROUP)
            ],
            axis=0,
        )
        den = jnp.sum(p, axis=-1, keepdims=True)
        o = mm(p.astype(bf16), v) * (1.0 / den)
        r = o[:AREA]
        for h in range(1, GROUP):
            r = jnp.where(lane_head == h, o[AREA * h : AREA * h + AREA], r)
        outs.append(r)
    return jnp.concatenate(outs, axis=1).astype(bf16)


def body(
    geo,
    lists_ref, place_ref, scale_ref, ids_ref, table_ref, book_ref, wq_hbm, wo_hbm, wc_hbm,
    out_ref,
    onehot, hid0, q0, k0, v0, att, hid1, q1, k1, v1, region, wq, wo, wc, sems,
):
    tr, tc, r0n, c0n, r1n, c1n, qr, qc, rr, width = geo
    copies = [
        pltpu.make_async_copy(wo_hbm, wo, sems.at[0]),
        pltpu.make_async_copy(wq_hbm.at[1], wq, sems.at[1]),
        pltpu.make_async_copy(wc_hbm, wc, sems.at[2]),
    ]
    for copy in copies:
        copy.start()
    own_r, own_c = place_ref[0], place_ref[1]
    r0, c0, r1, c1 = (place_ref[n] for n in range(2, 6))
    lane_head = lax.broadcasted_iota(i32, (1, HALF), 1) // HEAD
    ones_bd = (
        lax.broadcasted_iota(i32, (HALF, HALF), 0) // HEAD
        == lax.broadcasted_iota(i32, (HALF, HALF), 1) // HEAD
    ).astype(f32).astype(bf16)

    shift, digit = slot_tables()
    lanes = ids_ref.shape[1]
    place = lax.broadcasted_iota(i32, (AREA, lanes), 0)
    rel = (
        lax.broadcasted_iota(i32, (AREA, lanes), 1)
        - (place // TILE) % rr * width
        - place % TILE
    )
    packed = pack_digits(ids_ref[...])
    per_tile = TILE // rr
    for i in range(r1n):
        spread = jnp.concatenate(
            [
                jnp.broadcast_to(packed[n : n + 1], (TILE * rr, lanes))
                for n in range(i * per_tile, (i + 1) * per_tile)
            ],
            axis=0,
        )
        for j in range(c1n):
            mine = jnp.where(rel == TILE * (c1 + j), spread, 0.0)
            code = jnp.sum(mine, axis=-1, keepdims=True).astype(i32)
            hit = (lax.shift_right_logical(jnp.broadcast_to(code, (AREA, 128)), shift) & 7) == digit
            t = i * c1n + j
            onehot[AREA * t : AREA * t + AREA, :] = hit.astype(f32).astype(bf16)

    step1 = tiles_at_once(r1n * c1n)
    chunk1 = step1 * AREA

    def project0(n, _):
        rows = pl.ds(pl.multiple_of(n * chunk1, chunk1), chunk1)
        oh = onehot[rows, :]
        hid = mm(oh, book_ref[...]).astype(bf16)
        hid0[rows, :] = hid
        ms = square_mean(hid.astype(f32)) + norm_eps
        floor = norm_eps * ms
        q0[rows, :] = head_scale(mm(oh, table_ref[:, :D]), ones_bd, floor)
        k0[rows, :] = head_scale(mm(oh, table_ref[:, D : 2 * D]), ones_bd, floor)
        v0[rows, :] = (mm(oh, table_ref[:, 2 * D :]) * lax.rsqrt(ms)).astype(bf16)
        return 0

    lax.fori_loop(0, r1n * c1n // step1, project0, 0)

    bias_tile = lax.broadcasted_iota(i32, (1, NSEL * AREA), 1) // AREA

    def neighbours(gi, gj, row0, col0, cols):
        gi = jnp.clip(gi, 0, tr - 1)
        gj = jnp.clip(gj, 0, tc - 1)
        owner = gi // qr * (tc // qc) + gj // qc
        at = (gi % qr * qc + gj % qc) * NSEL
        starts = []
        bias = jnp.zeros((1, NSEL * AREA), f32)
        for n in range(NSEL):
            number = lists_ref[owner, at + n]
            ni = gi - 1 + number // 3
            nj = gj - 1 + number % 3
            inside = (ni >= 0) & (ni < tr) & (nj >= 0) & (nj < tc)
            ni = jnp.where(inside, ni, gi)
            nj = jnp.where(inside, nj, gj)
            starts.append(pl.multiple_of(((ni - row0) * cols + nj - col0) * AREA, AREA))
            bias = jnp.where(bias_tile == n, jnp.where(inside, 0.0, NEG), bias)
        return starts, bias

    def factors_of(layer):
        return [scale_ref[layer, h] * (LOG2E / math.sqrt(HEAD)) for h in range(HEADS)]

    fac0 = factors_of(0)

    def in_window0(t):
        return ((r0 - r1 + t // c0n) * c1n + (c0 - c1 + t % c0n)) * AREA

    step0 = tiles_at_once(r0n * c0n)
    chunk0 = step0 * AREA

    def attend0(m, _):
        for u in range(step0):
            t = m * step0 + u
            gi, gj = r0 + t // c0n, c0 + t % c0n
            starts, bias = neighbours(gi, gj, r1, c1, c1n)
            q = q0[pl.ds(pl.multiple_of(in_window0(t), AREA), AREA), :]
            att[pl.ds(pl.multiple_of(t * AREA, AREA), AREA), :] = attend_tile(
                q, starts, bias, fac0, k0, v0, lane_head
            )
        return 0

    lax.fori_loop(0, r0n * c0n // step0, attend0, 0)

    copies[0].wait()
    copies[1].wait()

    def project1(n, _):
        rows = pl.ds(pl.multiple_of(n * chunk0, chunk0), chunk0)
        old = jnp.concatenate(
            [
                hid0[pl.ds(pl.multiple_of(in_window0(n * step0 + u), AREA), AREA), :]
                for u in range(step0)
            ],
            axis=0,
        )
        hid = (old.astype(f32) + mm(att[rows, :], wo[0])).astype(bf16)
        hid1[rows, :] = hid
        ms = square_mean(hid.astype(f32)) + norm_eps
        floor = norm_eps * ms
        q1[rows, :] = head_scale(mm(hid, wq[:, :D]), ones_bd, floor)
        k1[rows, :] = head_scale(mm(hid, wq[:, D : 2 * D]), ones_bd, floor)
        v1[rows, :] = (mm(hid, wq[:, 2 * D :]) * lax.rsqrt(ms)).astype(bf16)
        return 0

    lax.fori_loop(0, r0n * c0n // step0, project1, 0)

    fac1 = factors_of(1)
    ring_r, ring_c = qr + 2, qc + 2

    def ring_row(i, _):
        gi = own_r - 1 + i
        for j in range(ring_c):
            gj = own_c - 1 + j
            starts, bias = neighbours(gi, gj, r0, c0, c0n)
            ci = jnp.clip(gi, 0, tr - 1)
            cj = jnp.clip(gj, 0, tc - 1)
            here = pl.ds(pl.multiple_of(((ci - r0) * c0n + cj - c0) * AREA, AREA), AREA)
            tile = attend_tile(q1[here, :], starts, bias, fac1, k1, v1, lane_head)
            att[pl.ds(pl.multiple_of((i * ring_c + j) * AREA, AREA), AREA), :] = tile
        return 0

    lax.fori_loop(0, ring_r, ring_row, 0)

    def finish_row(i, _):
        gi = own_r - 1 + i
        for j in range(ring_c):
            gj = own_c - 1 + j
            inside = (gi >= 0) & (gi < tr) & (gj >= 0) & (gj < tc)
            ci = jnp.clip(gi, 0, tr - 1)
            cj = jnp.clip(gj, 0, tc - 1)
            here = pl.ds(pl.multiple_of(((ci - r0) * c0n + cj - c0) * AREA, AREA), AREA)
            tile = att[pl.ds(pl.multiple_of((i * ring_c + j) * AREA, AREA), AREA), :]
            hid = (hid1[here, :].astype(f32) + mm(tile, wo[1])).astype(bf16).astype(f32)
            v = hid * lax.rsqrt(square_mean(hid) + norm_eps)
            act = jnp.where(inside, v / (1.0 + jnp.exp(-v)), 0.0)
            for r in range(TILE):
                region[pl.ds(i * TILE + r, 1), TILE * j : TILE * j + TILE, :] = act[
                    TILE * r : TILE * r + TILE
                ][None]
        return 0

    lax.fori_loop(0, ring_r, finish_row, 0)

    copies[2].wait()
    rows, cols = qr * TILE, qc * TILE
    total = jnp.zeros((rows * cols, wc.shape[-1]), f32)
    for dc in range(3):
        left = TILE - 1 + dc
        shifted = region[TILE - 1 : TILE + rows + 1, left : left + cols, :].astype(bf16)
        for dr in range(3):
            piece = shifted[dr : dr + rows].reshape(rows * cols, D)
            total = total + mm(piece, wc[dr, dc])
    out_ref[...] = total.astype(bf16).reshape(rows, cols, wc.shape[-1])


def table_body(book_ref, w_ref, table_ref, padded_ref):
    book = book_ref[...]
    full = mm(book, w_ref[0])
    high = full.astype(bf16)
    low = (full - high.astype(f32)).astype(bf16)
    table_ref[...] = jnp.concatenate([high, low], axis=0)
    padded_ref[...] = jnp.concatenate([book, jnp.zeros_like(book)], axis=0)


def local(token_ids, neighbour_lists, codebook, qkv_weight, out_weight, logit_scale, conv_weight):
    across = lax.axis_size("wa")
    down = lax.axis_size("ha")
    rr, width = token_ids.shape
    qr, qc = neighbour_lists.shape[:2]
    tr, tc = qr * down, qc * across
    assert TILE % rr == 0
    ids = token_ids.reshape(1, rr * width)
    lists = neighbour_lists.reshape(1, -1)
    id_lanes = -(-ids.shape[1] // 128) * 128
    list_lanes = -(-lists.shape[1] // 128) * 128
    row = jnp.concatenate(
        [
            jnp.pad(ids, ((0, 0), (0, id_lanes - ids.shape[1]))),
            jnp.pad(lists, ((0, 0), (0, list_lanes - lists.shape[1]))),
        ],
        axis=1,
    )
    group = down * across
    everyone = lax.all_to_all(
        jnp.broadcast_to(row, (group, row.shape[1])), ("ha", "wa"), 0, 0, tiled=True
    )

    own_r = lax.axis_index("ha") * qr
    own_c = lax.axis_index("wa") * qc
    r0n, c0n = min(qr + 4, tr), min(qc + 4, tc)
    r1n, c1n = min(r0n + 2, tr), min(c0n + 2, tc)
    r0 = jnp.clip(own_r - 2, 0, tr - r0n)
    c0 = jnp.clip(own_c - 2, 0, tc - c0n)
    r1 = jnp.clip(r0 - 1, 0, tr - r1n)
    c1 = jnp.clip(c0 - 1, 0, tc - c1n)
    place = jnp.stack([own_r, own_c, r0, c0, r1, c1]).astype(i32)
    id_rows = r1n * TILE // rr
    window = everyone
    if id_rows != group:
        window = lax.dynamic_slice_in_dim(everyone, r1 * TILE // rr, id_rows, axis=0)

    book = jnp.pad(codebook, ((0, 64 - codebook.shape[0]), (0, 0)))
    vmem = pl.BlockSpec(memory_space=pltpu.VMEM)
    smem = pl.BlockSpec(memory_space=pltpu.SMEM)
    hbm = pl.BlockSpec(memory_space=pl.ANY)
    table, padded = pl.pallas_call(
        table_body,
        out_shape=(
            jax.ShapeDtypeStruct((128, 3 * D), bf16),
            jax.ShapeDtypeStruct((128, D), bf16),
        ),
        grid=(1,),
        in_specs=[
            pl.BlockSpec((64, D), lambda n: (0, 0)),
            pl.BlockSpec((1, D, 3 * D), lambda n: (0, 0, 0)),
        ],
        out_specs=(
            pl.BlockSpec((128, 3 * D), lambda n: (0, 0)),
            pl.BlockSpec((128, D), lambda n: (0, 0)),
        ),
        name="tables",
    )(book, qkv_weight)

    n1, n0 = r1n * c1n * AREA, r0n * c0n * AREA
    natt = max(r0n * c0n, (qr + 2) * (qc + 2)) * AREA
    geo = (tr, tc, r0n, c0n, r1n, c1n, qr, qc, rr, width)
    cout = conv_weight.shape[3]
    return pl.pallas_call(
        functools.partial(body, geo),
        out_shape=jax.ShapeDtypeStruct((qr * TILE, qc * TILE, cout), bf16),
        grid=(1,),
        in_specs=[
            pl.BlockSpec((group, list_lanes), lambda n: (0, id_lanes // list_lanes), memory_space=pltpu.SMEM),
            smem, smem,
            pl.BlockSpec((id_rows, id_lanes), lambda n: (0, 0)),
            vmem, vmem, hbm, hbm, hbm,
        ],
        out_specs=pl.BlockSpec((qr * TILE, qc * TILE, cout), lambda n: (0, 0, 0)),
        scratch_shapes=[
            pltpu.VMEM((n1, 128), bf16),
            pltpu.VMEM((n1, D), bf16),
            pltpu.VMEM((n1, D), bf16),
            pltpu.VMEM((n1, D), bf16),
            pltpu.VMEM((n1, D), bf16),
            pltpu.VMEM((natt, D), bf16),
            pltpu.VMEM((n0, D), bf16),
            pltpu.VMEM((n0, D), bf16),
            pltpu.VMEM((n0, D), bf16),
            pltpu.VMEM((n0, D), bf16),
            pltpu.VMEM(((qr + 2) * TILE, (qc + 2) * TILE, D), f32),
            pltpu.VMEM((D, 3 * D), bf16),
            pltpu.VMEM((BLOCKS, D, D), bf16),
            pltpu.VMEM((3, 3, D, cout), bf16),
            pltpu.SemaphoreType.DMA((3,)),
        ],
        name="decode",
    )(everyone, place, logit_scale, window, table, padded, qkv_weight, out_weight, conv_weight)


def solution(mesh):
    in_specs = (
        P(("parts", "ha", "wa"), None),
        P(("parts", "ha"), "wa", None),
        P(),
        P(),
        P(),
        P(),
        P(),
    )
    out_specs = P(("parts", "ha"), "wa", None)
    return jax.shard_map(local, mesh=mesh, in_specs=in_specs, out_specs=out_specs, check_vma=False)
```

```python
import functools
import math

import jax
import jax.numpy as jnp
from jax import lax
from jax.experimental import pallas as pl
from jax.experimental.pallas import tpu as pltpu
from jax.sharding import PartitionSpec as P

D = 512
HEADS = 8
HEAD = D // HEADS
TILE = 8
AREA = TILE * TILE
NSEL = 6
BLOCKS = 2
HALF = 256
GROUP = HALF // HEAD
digit_levels = (8, 8, 8, 5, 5, 5)
digit_shift = (6, 3, 0, 9, 12, 15)
norm_eps = 1e-06
LOG2E = math.log2(math.e)
NEG = -1e30

f32 = jnp.float32
bf16 = jnp.bfloat16
i32 = jnp.int32


def mm(a, b):
    return lax.dot_general(a, b, (((1,), (0,)), ((), ())), preferred_element_type=f32)


def mm_t(a, b):
    return lax.dot_general(a, b, (((1,), (1,)), ((), ())), preferred_element_type=f32)


def span(count, size, total):
    return jnp.clip(count, 0, total - size)


def reach(starts, size, total):
    return max(min(s + size + 1, total) - max(s - 1, 0) for s in starts)


def pack_digits(ids):
    x = ids.astype(f32)
    q5 = jnp.floor((x + 0.5) * 0.2)
    q4 = jnp.floor((q5 + 0.5) * 0.2)
    q3 = jnp.floor((q4 + 0.5) * 0.2)
    return q3 + 512.0 * (q4 - 5.0 * q3) + 4096.0 * (q5 - 5.0 * q4) + 32768.0 * (x - 5.0 * q5)


def slot_tables():
    lane = lax.broadcasted_iota(i32, (1, 128), 1)
    slot = lane & 63
    shift = jnp.zeros_like(lane)
    start = jnp.zeros_like(lane)
    offset = 0
    for size, bits in zip(digit_levels, digit_shift):
        here = slot >= offset
        shift = jnp.where(here, bits, shift)
        start = jnp.where(here, offset, start)
        offset += size
    return shift, jnp.where(slot < offset, slot - start, -1)


def head_scale(x, ones_bd, floor):
    parts = []
    for half in range(D // HALF):
        piece = x[:, HALF * half : HALF * half + HALF]
        total = mm((piece * piece).astype(bf16), ones_bd)
        parts.append((piece * lax.rsqrt(total * (1.0 / HEAD) + floor)).astype(bf16))
    return jnp.concatenate(parts, axis=1)


def square_mean(x):
    return jnp.sum(x * x, axis=-1, keepdims=True) * (1.0 / D)


def attend_tile(q, starts, bias, factors, keys, values, lane_head):
    outs = []
    for g in range(D // HALF):
        cols = slice(HALF * g, HALF * g + HALF)
        qg = q[:, cols]
        q_bd = jnp.concatenate(
            [jnp.where(lane_head == h, qg, jnp.zeros_like(qg)) for h in range(GROUP)], axis=0
        )
        k = jnp.concatenate([keys[pl.ds(s, AREA), cols] for s in starts], axis=0)
        v = jnp.concatenate([values[pl.ds(s, AREA), cols] for s in starts], axis=0)
        s = mm_t(q_bd, k) + bias
        s = s - jnp.max(s, axis=-1, keepdims=True)
        p = jnp.concatenate(
            [
                jnp.exp2(s[AREA * h : AREA * h + AREA] * factors[GROUP * g + h])
                for h in range(GROUP)
            ],
            axis=0,
        )
        den = jnp.sum(p, axis=-1, keepdims=True)
        o = mm(p.astype(bf16), v) * (1.0 / den)
        r = o[:AREA]
        for h in range(1, GROUP):
            r = jnp.where(lane_head == h, o[AREA * h : AREA * h + AREA], r)
        outs.append(r)
    return jnp.concatenate(outs, axis=1).astype(bf16)


def attend_strip(q, starts, bias, factors, keys, values):
    count = q.shape[0]
    lane_head = lax.broadcasted_iota(i32, (1, D), 1) // HEAD
    q_bd = jnp.concatenate(
        [jnp.where(lane_head == h, q, jnp.zeros_like(q)) for h in range(HEADS)], axis=0
    )
    k = jnp.concatenate([keys[pl.ds(s, AREA), :] for s in starts], axis=0)
    v = jnp.concatenate([values[pl.ds(s, AREA), :] for s in starts], axis=0)
    s = mm_t(q_bd, k) + bias
    s = s - jnp.max(s, axis=-1, keepdims=True)
    p = jnp.concatenate(
        [jnp.exp2(s[count * h : count * h + count] * factors[h]) for h in range(HEADS)], axis=0
    )
    den = jnp.sum(p, axis=-1, keepdims=True)
    o = mm(p.astype(bf16), v) * (1.0 / den)
    r = o[:count]
    for h in range(1, HEADS):
        r = jnp.where(lane_head == h, o[count * h : count * h + count], r)
    return r.astype(bf16)


def block_ones():
    return (
        lax.broadcasted_iota(i32, (HALF, HALF), 0) // HEAD
        == lax.broadcasted_iota(i32, (HALF, HALF), 1) // HEAD
    ).astype(f32).astype(bf16)


def factors_of(scale_ref, layer):
    return [scale_ref[layer, h] * (LOG2E / math.sqrt(HEAD)) for h in range(HEADS)]


def rows_at(tile, count=AREA):
    return pl.ds(pl.multiple_of(tile * AREA, AREA), count)


def neighbours(geo, lists_ref, gi, gj, row0, col0, cols):
    gi = jnp.clip(gi, 0, geo.tr - 1)
    gj = jnp.clip(gj, 0, geo.tc - 1)
    owner = gi // geo.qr * (geo.tc // geo.qc) + gj // geo.qc
    at = geo.rr + gi % geo.qr * geo.qc + gj % geo.qc
    bias_tile = lax.broadcasted_iota(i32, (1, NSEL * AREA), 1) // AREA
    starts = []
    bias = jnp.zeros((1, NSEL * AREA), f32)
    for n in range(NSEL):
        number = lists_ref[owner, at, n]
        ni = gi - 1 + number // 3
        nj = gj - 1 + number % 3
        inside = (ni >= 0) & (ni < geo.tr) & (nj >= 0) & (nj < geo.tc)
        ni = jnp.where(inside, ni, gi)
        nj = jnp.where(inside, nj, gj)
        starts.append(pl.multiple_of(((ni - row0) * cols + nj - col0) * AREA, AREA))
        bias = jnp.where(bias_tile == n, jnp.where(inside, 0.0, NEG), bias)
    return starts, bias


class Geometry:
    def __init__(self, rr, width, qr, qc, down, across):
        self.rr, self.width, self.qr, self.qc = rr, width, qr, qc
        self.tr, self.tc = qr * down, qc * across
        self.sides = 2 if down % 2 == 0 else 1
        pair = qr * self.sides
        self.r0n = min(pair + 4, self.tr)
        if self.r0n % self.sides:
            self.sides, pair = 1, qr
            self.r0n = min(pair + 4, self.tr)
        self.pair = pair
        self.half = self.r0n // self.sides
        self.c0n = min(qc + 4, self.tc)
        clip = lambda at, size, total: min(max(at, 0), total - size)
        self.c1n = reach(
            [clip(n * qc - 2, self.c0n, self.tc) for n in range(across)], self.c0n, self.tc
        )
        self.r1n = reach(
            [
                clip(n * pair - 2, self.r0n, self.tr) + side * self.half
                for n in range(self.tr // pair)
                for side in range(self.sides)
            ],
            self.half,
            self.tr,
        )

    def place(self):
        ha, wa = lax.axis_index("ha"), lax.axis_index("wa")
        own_r, own_c = ha * self.qr, wa * self.qc
        side = ha % self.sides
        p0 = span(ha // self.sides * self.pair - 2, self.r0n, self.tr)
        c0 = span(own_c - 2, self.c0n, self.tc)
        r0 = p0 + side * self.half
        r1 = span(r0 - 1, self.r1n, self.tr)
        c1 = span(c0 - 1, self.c1n, self.tc)
        return own_r, own_c, side, p0, r0, c0, r1, c1


def first_body(
    geo,
    lists_ref, scale_ref, ids_ref, table_ref, book_ref, wq_hbm, wo_hbm, wc_hbm,
    out_ref, wq1_ref, wo1_ref, wc_ref,
    onehot, floors, hid0, q0, k0, v0, att, wo, sems,
):
    copies = [
        pltpu.make_async_copy(wo_hbm.at[0], wo, sems.at[0]),
        pltpu.make_async_copy(wq_hbm.at[1], wq1_ref, sems.at[1]),
        pltpu.make_async_copy(wo_hbm.at[1], wo1_ref, sems.at[2]),
        pltpu.make_async_copy(wc_hbm, wc_ref, sems.at[3]),
    ]
    for copy in copies:
        copy.start()
    own_r, own_c, side, p0, r0, c0, r1, c1 = geo.place()
    c0n, c1n, rr = geo.c0n, geo.c1n, geo.rr
    lane_head = lax.broadcasted_iota(i32, (1, HALF), 1) // HEAD
    ones_bd = block_ones()

    shift, digit = slot_tables()
    lanes = ids_ref.shape[2]
    rel = (
        lax.broadcasted_iota(i32, (AREA, lanes), 1)
        - lax.broadcasted_iota(i32, (AREA, lanes), 0) % TILE
    )
    per_tile = TILE // rr
    for i in range(geo.r1n):
        rows = []
        for n in range(per_tile):
            packed = pack_digits(ids_ref[(r1 + i) * per_tile + n])
            rows += [jnp.broadcast_to(packed[r : r + 1], (TILE, lanes)) for r in range(rr)]
        spread = jnp.concatenate(rows, axis=0)
        for j in range(c1n):
            mine = jnp.where(rel == TILE * (c1 + j), spread, 0.0)
            code = jnp.sum(mine, axis=-1, keepdims=True).astype(i32)
            hit = (lax.shift_right_logical(jnp.broadcast_to(code, (AREA, 128)), shift) & 7) == digit
            t = i * c1n + j
            onehot[AREA * t : AREA * t + AREA, :] = hit.astype(f32).astype(bf16)

    def project_keys(i, _):
        rows = rows_at(i * c1n, c1n * AREA)
        oh = onehot[rows, :]
        hid = mm(oh, book_ref[...]).astype(bf16)
        hid0[rows, :] = hid
        ms = square_mean(hid.astype(f32)) + norm_eps
        floor = norm_eps * ms
        floors[rows, :] = floor
        k0[rows, :] = head_scale(mm(oh, table_ref[:, D : 2 * D]), ones_bd, floor)
        v0[rows, :] = (mm(oh, table_ref[:, 2 * D :]) * lax.rsqrt(ms)).astype(bf16)
        return 0

    lax.fori_loop(0, geo.r1n, project_keys, 0)

    def in_window(i):
        return rows_at((r0 - r1 + i) * c1n + c0 - c1, c0n * AREA)

    def project_queries(i, _):
        rows = in_window(i)
        q = mm(onehot[rows, :], table_ref[:, :D])
        q0[rows_at(i * c0n, c0n * AREA), :] = head_scale(q, ones_bd, floors[rows, :])
        return 0

    lax.fori_loop(0, geo.half, project_queries, 0)

    factors = factors_of(scale_ref, 0)

    def attend(i, _):
        for j in range(c0n):
            starts, bias = neighbours(geo, lists_ref, r0 + i, c0 + j, r1, c1, c1n)
            here = rows_at(i * c0n + j)
            att[here, :] = attend_tile(q0[here, :], starts, bias, factors, k0, v0, lane_head)
        return 0

    lax.fori_loop(0, geo.half, attend, 0)

    copies[0].wait()

    def project_out(i, _):
        rows = rows_at(i * c0n, c0n * AREA)
        old = hid0[in_window(i), :].astype(f32)
        out_ref[rows, :] = (old + mm(att[rows, :], wo[...])).astype(bf16)
        return 0

    lax.fori_loop(0, geo.half, project_out, 0)
    for copy in copies[1:]:
        copy.wait()


STRIP = 16


def second_body(
    geo,
    lists_ref, scale_ref, own_ref, other_ref, wq, wo, wc,
    out_ref,
    hid, k1, v1, queries, q1, att, region,
):
    own_r, own_c, side, p0, r0, c0, r1, c1 = geo.place()
    c0n, qr, qc = geo.c0n, geo.qr, geo.qc
    half = geo.half * c0n
    hid[rows_at(side * half, half * AREA), :] = own_ref[...]
    if geo.sides == 2:
        hid[rows_at((1 - side) * half, half * AREA), :] = other_ref[...]
    lane_head = lax.broadcasted_iota(i32, (1, HALF), 1) // HEAD
    ones_bd = block_ones()

    def project_keys(i, _):
        rows = rows_at(i * c0n, c0n * AREA)
        h = hid[rows, :]
        ms = square_mean(h.astype(f32)) + norm_eps
        k1[rows, :] = head_scale(mm(h, wq[:, D : 2 * D]), ones_bd, norm_eps * ms)
        v1[rows, :] = (mm(h, wq[:, 2 * D :]) * lax.rsqrt(ms)).astype(bf16)
        return 0

    lax.fori_loop(0, geo.r0n, project_keys, 0)

    ring = qc + 2

    def clipped(gi, gj):
        ci = jnp.clip(gi, 0, geo.tr - 1)
        cj = jnp.clip(gj, 0, geo.tc - 1)
        return (ci - p0) * c0n + cj - c0

    whole = [(own_r + i, own_c - 1 + j) for i in range(qr) for j in range(ring)]
    strips = [(own_r - 1, own_c - 1 + j, AREA - STRIP) for j in range(ring)]
    strips += [(own_r + qr, own_c - 1 + j, 0) for j in range(ring)]
    base = len(whole) * AREA
    for n, (gi, gj) in enumerate(whole):
        queries[AREA * n : AREA * n + AREA, :] = hid[rows_at(clipped(gi, gj)), :]
    for n, (gi, gj, skip) in enumerate(strips):
        at = base + STRIP * n
        here = pl.ds(pl.multiple_of(clipped(gi, gj) * AREA + skip, STRIP), STRIP)
        queries[at : at + STRIP, :] = hid[here, :]
    h = queries[...]
    ms = square_mean(h.astype(f32)) + norm_eps
    q1[...] = head_scale(mm(h, wq[:, :D]), ones_bd, norm_eps * ms)

    factors = factors_of(scale_ref, 1)
    for n, (gi, gj) in enumerate(whole):
        starts, bias = neighbours(geo, lists_ref, gi, gj, p0, c0, c0n)
        at = slice(AREA * n, AREA * n + AREA)
        att[at, :] = attend_tile(q1[at, :], starts, bias, factors, k1, v1, lane_head)
    for n, (gi, gj, _) in enumerate(strips):
        starts, bias = neighbours(geo, lists_ref, gi, gj, p0, c0, c0n)
        at = slice(base + STRIP * n, base + STRIP * n + STRIP)
        att[at, :] = attend_strip(q1[at, :], starts, bias, factors, k1, v1)

    h = (queries[...].astype(f32) + mm(att[...], wo[...])).astype(bf16).astype(f32)
    v = h * lax.rsqrt(square_mean(h) + norm_eps)
    act = v / (1.0 + jnp.exp(-v))

    def kept(piece, gi, gj):
        inside = (gi >= 0) & (gi < geo.tr) & (gj >= 0) & (gj < geo.tc)
        return jnp.where(inside, piece, 0.0)

    for n, (gi, gj) in enumerate(whole):
        i, j = divmod(n, ring)
        tile = kept(act[AREA * n : AREA * n + AREA], gi, gj)
        for r in range(TILE):
            region[1 + TILE * i + r, TILE * j : TILE * j + TILE, :] = tile[TILE * r : TILE * r + TILE]
    for n, (gi, gj, skip) in enumerate(strips):
        i, j = divmod(n, ring)
        at = base + STRIP * n + (STRIP - TILE if skip else 0)
        row = (qr * TILE + 1) * i
        region[row, TILE * j : TILE * j + TILE, :] = kept(act[at : at + TILE], gi, gj)

    rows, cols = qr * TILE, qc * TILE
    total = jnp.zeros((rows * cols, wc.shape[-1]), f32)
    for dc in range(3):
        left = TILE - 1 + dc
        shifted = region[:, left : left + cols, :].astype(bf16)
        for dr in range(3):
            piece = shifted[dr : dr + rows].reshape(rows * cols, D)
            total = total + mm(piece, wc[dr, dc])
    out_ref[...] = total.astype(bf16).reshape(rows, cols, wc.shape[-1])


def table_body(book_ref, wq_hbm, table_ref, padded_ref, wq, sem):
    copy = pltpu.make_async_copy(wq_hbm.at[0], wq, sem)
    copy.start()
    book = jnp.concatenate(
        [book_ref[...].astype(f32), jnp.zeros((64 - book_ref.shape[0], D), f32)], axis=0
    ).astype(bf16)
    copy.wait()
    full = mm(book, wq[...])
    high = full.astype(bf16)
    low = (full - high.astype(f32)).astype(bf16)
    table_ref[...] = jnp.concatenate([high, low], axis=0)
    padded_ref[...] = jnp.concatenate([book, jnp.zeros_like(book)], axis=0)


VMEM_LIMIT = 20 << 20


def on_chip(x):
    return pltpu.with_memory_space_constraint(x, pltpu.VMEM)


def off_chip(x):
    return pltpu.with_memory_space_constraint(x, pltpu.HBM)


vmem = pl.BlockSpec(memory_space=pltpu.VMEM)
hbm = pl.BlockSpec(memory_space=pltpu.HBM)
smem = pl.BlockSpec(memory_space=pltpu.SMEM)


def local(token_ids, neighbour_lists, codebook, qkv_weight, out_weight, logit_scale, conv_weight):
    across = lax.axis_size("wa")
    down = lax.axis_size("ha")
    rr, width = token_ids.shape
    qr, qc = neighbour_lists.shape[:2]
    assert TILE % rr == 0
    geo = Geometry(rr, width, qr, qc, down, across)
    lists = neighbour_lists.reshape(qr * qc, NSEL)
    lanes = -(-width // 128) * 128
    mine = jnp.concatenate(
        [
            jnp.pad(token_ids, ((0, 0), (0, lanes - width))),
            jnp.pad(lists, ((0, 0), (0, lanes - NSEL))),
        ],
        axis=0,
    )
    everyone = lax.all_to_all(
        jnp.broadcast_to(mine, (down * across,) + mine.shape), ("ha", "wa"), 0, 0, tiled=True
    )

    table, padded = pl.pallas_call(
        table_body,
        out_shape=(pltpu.VMEM((128, 3 * D), bf16), pltpu.VMEM((128, D), bf16)),
        in_specs=[vmem, hbm],
        out_specs=(vmem, vmem),
        scratch_shapes=[pltpu.VMEM((D, 3 * D), bf16), pltpu.SemaphoreType.DMA],
        compiler_params=pltpu.CompilerParams(vmem_limit_bytes=VMEM_LIMIT),
        name="tables",
    )(codebook, off_chip(qkv_weight))

    n1 = geo.r1n * geo.c1n * AREA
    nh = geo.half * geo.c0n * AREA
    cout = conv_weight.shape[3]
    own, wq1, wo1, wc = pl.pallas_call(
        functools.partial(first_body, geo),
        out_shape=(
            pltpu.VMEM((nh, D), bf16),
            pltpu.VMEM((D, 3 * D), bf16),
            pltpu.VMEM((D, D), bf16),
            pltpu.VMEM((3, 3, D, cout), bf16),
        ),
        in_specs=[smem, smem, vmem, vmem, vmem, hbm, hbm, hbm],
        out_specs=(vmem,) * 4,
        scratch_shapes=[
            pltpu.VMEM((n1, 128), bf16),
            pltpu.VMEM((n1, 1), f32),
            pltpu.VMEM((n1, D), bf16),
            pltpu.VMEM((nh, D), bf16),
            pltpu.VMEM((n1, D), bf16),
            pltpu.VMEM((n1, D), bf16),
            pltpu.VMEM((nh, D), bf16),
            pltpu.VMEM((D, D), bf16),
            pltpu.SemaphoreType.DMA((4,)),
        ],
        compiler_params=pltpu.CompilerParams(vmem_limit_bytes=VMEM_LIMIT),
        name="first",
    )(
        everyone, logit_scale, everyone, on_chip(table), on_chip(padded),
        *map(off_chip, (qkv_weight, out_weight, conv_weight)),
    )
    other = own
    if geo.sides == 2:
        other = lax.ppermute(own, "ha", [(n, n ^ 1) for n in range(down)])

    n0 = geo.r0n * geo.c0n * AREA
    nq = qr * (qc + 2) * AREA + 2 * (qc + 2) * STRIP
    return pl.pallas_call(
        functools.partial(second_body, geo),
        out_shape=jax.ShapeDtypeStruct((qr * TILE, qc * TILE, cout), bf16),
        in_specs=[smem, smem, vmem, vmem, vmem, vmem, vmem],
        out_specs=vmem,
        scratch_shapes=[
            pltpu.VMEM((n0, D), bf16),
            pltpu.VMEM((n0, D), bf16),
            pltpu.VMEM((n0, D), bf16),
            pltpu.VMEM((nq, D), bf16),
            pltpu.VMEM((nq, D), bf16),
            pltpu.VMEM((nq, D), bf16),
            pltpu.VMEM((qr * TILE + 2, (qc + 2) * TILE, D), f32),
        ],
        compiler_params=pltpu.CompilerParams(vmem_limit_bytes=VMEM_LIMIT),
        name="second",
    )(everyone, logit_scale, *map(on_chip, (own, other, wq1, wo1, wc)))


def solution(mesh):
    in_specs = (
        P(("parts", "ha", "wa"), None),
        P(("parts", "ha"), "wa", None),
        P(),
        P(),
        P(),
        P(),
        P(),
    )
    out_specs = P(("parts", "ha"), "wa", None)
    return jax.shard_map(local, mesh=mesh, in_specs=in_specs, out_specs=out_specs, check_vma=False)
```

```python
import functools
import math

import jax
import jax.numpy as jnp
from jax import lax
from jax.experimental import pallas as pl
from jax.experimental.pallas import tpu as pltpu
from jax.sharding import PartitionSpec as P

D = 512
HEADS = 8
HEAD = D // HEADS
TILE = 8
AREA = TILE * TILE
NSEL = 6
BLOCKS = 2
HALF = 256
GROUP = HALF // HEAD
digit_levels = (8, 8, 8, 5, 5, 5)
digit_shift = (6, 3, 0, 9, 12, 15)
norm_eps = 1e-06
LOG2E = math.log2(math.e)
NEG = -1e30

f32 = jnp.float32
bf16 = jnp.bfloat16
i32 = jnp.int32


def mm(a, b):
    return lax.dot_general(a, b, (((1,), (0,)), ((), ())), preferred_element_type=f32)


def mm_t(a, b):
    return lax.dot_general(a, b, (((1,), (1,)), ((), ())), preferred_element_type=f32)


def span(count, size, total):
    return jnp.clip(count, 0, total - size)


def reach(starts, size, total):
    return max(min(s + size + 1, total) - max(s - 1, 0) for s in starts)


def pack_digits(ids):
    x = ids.astype(f32)
    q5 = jnp.floor((x + 0.5) * 0.2)
    q4 = jnp.floor((q5 + 0.5) * 0.2)
    q3 = jnp.floor((q4 + 0.5) * 0.2)
    return q3 + 512.0 * (q4 - 5.0 * q3) + 4096.0 * (q5 - 5.0 * q4) + 32768.0 * (x - 5.0 * q5)


def slot_tables():
    lane = lax.broadcasted_iota(i32, (1, 128), 1)
    slot = lane & 63
    shift = jnp.zeros_like(lane)
    start = jnp.zeros_like(lane)
    offset = 0
    for size, bits in zip(digit_levels, digit_shift):
        here = slot >= offset
        shift = jnp.where(here, bits, shift)
        start = jnp.where(here, offset, start)
        offset += size
    return shift, jnp.where(slot < offset, slot - start, -1)


def head_scale(x, ones_bd, floor):
    parts = []
    for half in range(D // HALF):
        piece = x[:, HALF * half : HALF * half + HALF]
        total = mm((piece * piece).astype(bf16), ones_bd)
        parts.append((piece * lax.rsqrt(total * (1.0 / HEAD) + floor)).astype(bf16))
    return jnp.concatenate(parts, axis=1)


def square_mean(x):
    return jnp.sum(x * x, axis=-1, keepdims=True) * (1.0 / D)


def attend_tile(q, starts, bias, factors, keys, values, lane_head):
    outs = []
    for g in range(D // HALF):
        cols = slice(HALF * g, HALF * g + HALF)
        qg = q[:, cols]
        q_bd = jnp.concatenate(
            [jnp.where(lane_head == h, qg, jnp.zeros_like(qg)) for h in range(GROUP)], axis=0
        )
        k = jnp.concatenate([keys[pl.ds(s, AREA), cols] for s in starts], axis=0)
        v = jnp.concatenate([values[pl.ds(s, AREA), cols] for s in starts], axis=0)
        s = mm_t(q_bd, k) + bias
        s = s - jnp.max(s, axis=-1, keepdims=True)
        p = jnp.concatenate(
            [
                jnp.exp2(s[AREA * h : AREA * h + AREA] * factors[GROUP * g + h])
                for h in range(GROUP)
            ],
            axis=0,
        )
        den = jnp.sum(p, axis=-1, keepdims=True)
        o = mm(p.astype(bf16), v) * (1.0 / den)
        r = o[:AREA]
        for h in range(1, GROUP):
            r = jnp.where(lane_head == h, o[AREA * h : AREA * h + AREA], r)
        outs.append(r)
    return jnp.concatenate(outs, axis=1).astype(bf16)


def attend_strip(q, starts, bias, factors, keys, values):
    count = q.shape[0]
    lane_head = lax.broadcasted_iota(i32, (1, D), 1) // HEAD
    q_bd = jnp.concatenate(
        [jnp.where(lane_head == h, q, jnp.zeros_like(q)) for h in range(HEADS)], axis=0
    )
    k = jnp.concatenate([keys[pl.ds(s, AREA), :] for s in starts], axis=0)
    v = jnp.concatenate([values[pl.ds(s, AREA), :] for s in starts], axis=0)
    s = mm_t(q_bd, k) + bias
    s = s - jnp.max(s, axis=-1, keepdims=True)
    p = jnp.concatenate(
        [jnp.exp2(s[count * h : count * h + count] * factors[h]) for h in range(HEADS)], axis=0
    )
    den = jnp.sum(p, axis=-1, keepdims=True)
    o = mm(p.astype(bf16), v) * (1.0 / den)
    r = o[:count]
    for h in range(1, HEADS):
        r = jnp.where(lane_head == h, o[count * h : count * h + count], r)
    return r.astype(bf16)


def block_ones():
    return (
        lax.broadcasted_iota(i32, (HALF, HALF), 0) // HEAD
        == lax.broadcasted_iota(i32, (HALF, HALF), 1) // HEAD
    ).astype(f32).astype(bf16)


def factors_of(scale_ref, layer):
    return [scale_ref[layer, h] * (LOG2E / math.sqrt(HEAD)) for h in range(HEADS)]


def rows_at(tile, count=AREA):
    return pl.ds(pl.multiple_of(tile * AREA, AREA), count)


def neighbours(geo, lists_ref, gi, gj, row0, col0, cols):
    gi = jnp.clip(gi, 0, geo.tr - 1)
    gj = jnp.clip(gj, 0, geo.tc - 1)
    owner = gi // geo.qr * (geo.tc // geo.qc) + gj // geo.qc
    at = gi % geo.qr * geo.qc + gj % geo.qc
    bias_tile = lax.broadcasted_iota(i32, (1, NSEL * AREA), 1) // AREA
    starts = []
    bias = jnp.zeros((1, NSEL * AREA), f32)
    for n in range(NSEL):
        number = lists_ref[owner, at, n]
        ni = gi - 1 + number // 3
        nj = gj - 1 + number % 3
        inside = (ni >= 0) & (ni < geo.tr) & (nj >= 0) & (nj < geo.tc)
        ni = jnp.where(inside, ni, gi)
        nj = jnp.where(inside, nj, gj)
        starts.append(pl.multiple_of(((ni - row0) * cols + nj - col0) * AREA, AREA))
        bias = jnp.where(bias_tile == n, jnp.where(inside, 0.0, NEG), bias)
    return starts, bias


class Geometry:
    def __init__(self, rr, width, qr, qc, down, across):
        self.rr, self.width, self.qr, self.qc = rr, width, qr, qc
        self.tr, self.tc = qr * down, qc * across
        self.sides = 2 if down % 2 == 0 else 1
        pair = qr * self.sides
        self.r0n = min(pair + 4, self.tr)
        if self.r0n % self.sides:
            self.sides, pair = 1, qr
            self.r0n = min(pair + 4, self.tr)
        self.pair = pair
        self.half = self.r0n // self.sides
        self.c0n = min(qc + 4, self.tc)
        clip = lambda at, size, total: min(max(at, 0), total - size)
        self.c1n = reach(
            [clip(n * qc - 2, self.c0n, self.tc) for n in range(across)], self.c0n, self.tc
        )
        self.r1n = reach(
            [
                clip(n * pair - 2, self.r0n, self.tr) + side * self.half
                for n in range(self.tr // pair)
                for side in range(self.sides)
            ],
            self.half,
            self.tr,
        )

    def place(self):
        ha, wa = lax.axis_index("ha"), lax.axis_index("wa")
        own_r, own_c = ha * self.qr, wa * self.qc
        side = ha % self.sides
        p0 = span(ha // self.sides * self.pair - 2, self.r0n, self.tr)
        c0 = span(own_c - 2, self.c0n, self.tc)
        r0 = p0 + side * self.half
        r1 = span(r0 - 1, self.r1n, self.tr)
        c1 = span(c0 - 1, self.c1n, self.tc)
        return own_r, own_c, side, p0, r0, c0, r1, c1


def first_body(
    geo,
    scale_hbm, ids_ref, table_ref, book_ref, wq_hbm, wo_hbm, wc_hbm,
    out_ref, wq1_ref, wo1_ref, wc_ref,
    lists_ref, scale_ref, onehot, floors, hid0, q0, k0, v0, att, wo, sems,
):
    copies = [
        pltpu.make_async_copy(ids_ref.at[:, pl.ds(geo.rr, geo.qr * geo.qc), :], lists_ref, sems.at[0]),
        pltpu.make_async_copy(scale_hbm, scale_ref, sems.at[1]),
        pltpu.make_async_copy(wo_hbm.at[0], wo, sems.at[2]),
        pltpu.make_async_copy(wq_hbm.at[1], wq1_ref, sems.at[3]),
        pltpu.make_async_copy(wo_hbm.at[1], wo1_ref, sems.at[4]),
        pltpu.make_async_copy(wc_hbm, wc_ref, sems.at[5]),
    ]
    for copy in copies:
        copy.start()
    own_r, own_c, side, p0, r0, c0, r1, c1 = geo.place()
    c0n, c1n, rr = geo.c0n, geo.c1n, geo.rr
    lane_head = lax.broadcasted_iota(i32, (1, HALF), 1) // HEAD
    ones_bd = block_ones()

    shift, digit = slot_tables()
    lanes = ids_ref.shape[2]
    rel = (
        lax.broadcasted_iota(i32, (AREA, lanes), 1)
        - lax.broadcasted_iota(i32, (AREA, lanes), 0) % TILE
    )
    per_tile = TILE // rr
    for i in range(geo.r1n):
        rows = []
        for n in range(per_tile):
            packed = pack_digits(ids_ref[(r1 + i) * per_tile + n])
            rows += [jnp.broadcast_to(packed[r : r + 1], (TILE, lanes)) for r in range(rr)]
        spread = jnp.concatenate(rows, axis=0)
        for j in range(c1n):
            mine = jnp.where(rel == TILE * (c1 + j), spread, 0.0)
            code = jnp.sum(mine, axis=-1, keepdims=True).astype(i32)
            hit = (lax.shift_right_logical(jnp.broadcast_to(code, (AREA, 128)), shift) & 7) == digit
            t = i * c1n + j
            onehot[AREA * t : AREA * t + AREA, :] = hit.astype(f32).astype(bf16)

    def project_keys(i, _):
        rows = rows_at(i * c1n, c1n * AREA)
        oh = onehot[rows, :]
        hid = mm(oh, book_ref[...]).astype(bf16)
        hid0[rows, :] = hid
        ms = square_mean(hid.astype(f32)) + norm_eps
        floor = norm_eps * ms
        floors[rows, :] = floor
        k0[rows, :] = head_scale(mm(oh, table_ref[:, D : 2 * D]), ones_bd, floor)
        v0[rows, :] = (mm(oh, table_ref[:, 2 * D :]) * lax.rsqrt(ms)).astype(bf16)
        return 0

    lax.fori_loop(0, geo.r1n, project_keys, 0)

    def in_window(i):
        return rows_at((r0 - r1 + i) * c1n + c0 - c1, c0n * AREA)

    def project_queries(i, _):
        rows = in_window(i)
        q = mm(onehot[rows, :], table_ref[:, :D])
        q0[rows_at(i * c0n, c0n * AREA), :] = head_scale(q, ones_bd, floors[rows, :])
        return 0

    lax.fori_loop(0, geo.half, project_queries, 0)

    copies[0].wait()
    copies[1].wait()
    factors = factors_of(scale_ref, 0)

    def attend(i, _):
        for j in range(c0n):
            starts, bias = neighbours(geo, lists_ref, r0 + i, c0 + j, r1, c1, c1n)
            here = rows_at(i * c0n + j)
            att[here, :] = attend_tile(q0[here, :], starts, bias, factors, k0, v0, lane_head)
        return 0

    lax.fori_loop(0, geo.half, attend, 0)

    copies[2].wait()

    def project_out(i, _):
        rows = rows_at(i * c0n, c0n * AREA)
        old = hid0[in_window(i), :].astype(f32)
        out_ref[rows, :] = (old + mm(att[rows, :], wo[...])).astype(bf16)
        return 0

    lax.fori_loop(0, geo.half, project_out, 0)
    for copy in copies[3:]:
        copy.wait()


def layer1_keys(hid, wq, ones_bd, rows, k1, v1):
    h = hid[rows, :]
    ms = square_mean(h.astype(f32)) + norm_eps
    k1[rows, :] = head_scale(mm(h, wq[:, D : 2 * D]), ones_bd, norm_eps * ms)
    v1[rows, :] = (mm(h, wq[:, 2 * D :]) * lax.rsqrt(ms)).astype(bf16)


def half_keys(geo, source, side, wq, hid, k1, v1):
    ones_bd = block_ones()
    step = geo.c0n
    first = side * geo.half

    def one(i, _):
        rows = rows_at((first + i) * step, step * AREA)
        hid[rows, :] = source[rows_at(i * step, step * AREA), :]
        layer1_keys(hid, wq, ones_bd, rows, k1, v1)
        return 0

    lax.fori_loop(0, geo.half, one, 0)


def own_keys_body(geo, own_ref, wq, hid, k1, v1):
    side = geo.place()[2]
    half_keys(geo, own_ref, side, wq, hid, k1, v1)


STRIP = 16


def second_body(
    geo,
    scale_hbm, ids_ref, other_ref, wq, wo, wc, hid_in, k1_in, v1_in,
    out_ref, hid, k1, v1,
    lists_ref, scale_ref, queries, q1, att, region, sems,
):
    copies = [
        pltpu.make_async_copy(ids_ref.at[:, pl.ds(geo.rr, geo.qr * geo.qc), :], lists_ref, sems.at[0]),
        pltpu.make_async_copy(scale_hbm, scale_ref, sems.at[1]),
    ]
    for copy in copies:
        copy.start()
    own_r, own_c, side, p0, r0, c0, r1, c1 = geo.place()
    c0n, qr, qc = geo.c0n, geo.qr, geo.qc
    lane_head = lax.broadcasted_iota(i32, (1, HALF), 1) // HEAD
    ones_bd = block_ones()
    if geo.sides == 2:
        half_keys(geo, other_ref, 1 - side, wq, hid, k1, v1)

    ring = qc + 2

    def clipped(gi, gj):
        ci = jnp.clip(gi, 0, geo.tr - 1)
        cj = jnp.clip(gj, 0, geo.tc - 1)
        return (ci - p0) * c0n + cj - c0

    whole = [(own_r + i, own_c - 1 + j) for i in range(qr) for j in range(ring)]
    strips = [(own_r - 1, own_c - 1 + j, AREA - STRIP) for j in range(ring)]
    strips += [(own_r + qr, own_c - 1 + j, 0) for j in range(ring)]
    base = len(whole) * AREA
    for n, (gi, gj) in enumerate(whole):
        queries[AREA * n : AREA * n + AREA, :] = hid[rows_at(clipped(gi, gj)), :]
    for n, (gi, gj, skip) in enumerate(strips):
        at = base + STRIP * n
        here = pl.ds(pl.multiple_of(clipped(gi, gj) * AREA + skip, STRIP), STRIP)
        queries[at : at + STRIP, :] = hid[here, :]
    h = queries[...]
    ms = square_mean(h.astype(f32)) + norm_eps
    q1[...] = head_scale(mm(h, wq[:, :D]), ones_bd, norm_eps * ms)

    for copy in copies:
        copy.wait()
    factors = factors_of(scale_ref, 1)
    for n, (gi, gj) in enumerate(whole):
        starts, bias = neighbours(geo, lists_ref, gi, gj, p0, c0, c0n)
        at = slice(AREA * n, AREA * n + AREA)
        att[at, :] = attend_tile(q1[at, :], starts, bias, factors, k1, v1, lane_head)
    for n, (gi, gj, _) in enumerate(strips):
        starts, bias = neighbours(geo, lists_ref, gi, gj, p0, c0, c0n)
        at = slice(base + STRIP * n, base + STRIP * n + STRIP)
        att[at, :] = attend_strip(q1[at, :], starts, bias, factors, k1, v1)

    h = (queries[...].astype(f32) + mm(att[...], wo[...])).astype(bf16).astype(f32)
    v = h * lax.rsqrt(square_mean(h) + norm_eps)
    act = v / (1.0 + jnp.exp(-v))

    def kept(piece, gi, gj):
        inside = (gi >= 0) & (gi < geo.tr) & (gj >= 0) & (gj < geo.tc)
        return jnp.where(inside, piece, 0.0)

    for n, (gi, gj) in enumerate(whole):
        i, j = divmod(n, ring)
        tile = kept(act[AREA * n : AREA * n + AREA], gi, gj)
        for r in range(TILE):
            region[1 + TILE * i + r, TILE * j : TILE * j + TILE, :] = tile[TILE * r : TILE * r + TILE]
    for n, (gi, gj, skip) in enumerate(strips):
        i, j = divmod(n, ring)
        at = base + STRIP * n + (STRIP - TILE if skip else 0)
        row = (qr * TILE + 1) * i
        region[row, TILE * j : TILE * j + TILE, :] = kept(act[at : at + TILE], gi, gj)

    rows, cols = qr * TILE, qc * TILE
    total = jnp.zeros((rows * cols, wc.shape[-1]), f32)
    for dc in range(3):
        left = TILE - 1 + dc
        shifted = region[:, left : left + cols, :].astype(bf16)
        for dr in range(3):
            piece = shifted[dr : dr + rows].reshape(rows * cols, D)
            total = total + mm(piece, wc[dr, dc])
    out_ref[...] = total.astype(bf16).reshape(rows, cols, wc.shape[-1])


def table_body(book_ref, wq_hbm, table_ref, padded_ref, wq, sem):
    copy = pltpu.make_async_copy(wq_hbm.at[0], wq, sem)
    copy.start()
    book = jnp.concatenate(
        [book_ref[...].astype(f32), jnp.zeros((64 - book_ref.shape[0], D), f32)], axis=0
    ).astype(bf16)
    copy.wait()
    full = mm(book, wq[...])
    high = full.astype(bf16)
    low = (full - high.astype(f32)).astype(bf16)
    table_ref[...] = jnp.concatenate([high, low], axis=0)
    padded_ref[...] = jnp.concatenate([book, jnp.zeros_like(book)], axis=0)


VMEM_LIMIT = 20 << 20


def on_chip(x):
    return pltpu.with_memory_space_constraint(x, pltpu.VMEM)


def off_chip(x):
    return pltpu.with_memory_space_constraint(x, pltpu.HBM)


vmem = pl.BlockSpec(memory_space=pltpu.VMEM)
hbm = pl.BlockSpec(memory_space=pltpu.HBM)


def local(token_ids, neighbour_lists, codebook, qkv_weight, out_weight, logit_scale, conv_weight):
    across = lax.axis_size("wa")
    down = lax.axis_size("ha")
    rr, width = token_ids.shape
    qr, qc = neighbour_lists.shape[:2]
    assert TILE % rr == 0
    geo = Geometry(rr, width, qr, qc, down, across)
    lists = neighbour_lists.reshape(qr * qc, NSEL)
    lanes = -(-width // 128) * 128
    group = down * across
    count = rr + qr * qc
    mine = jnp.pad(
        jnp.broadcast_to(token_ids, (group, rr, width)), ((0, 0), (0, count - rr), (0, lanes - width))
    ) + jnp.pad(
        jnp.broadcast_to(lists, (group, qr * qc, NSEL)), ((0, 0), (rr, 0), (0, lanes - NSEL))
    )
    everyone = lax.all_to_all(mine, ("ha", "wa"), 0, 0, tiled=True)

    table, padded = pl.pallas_call(
        table_body,
        out_shape=(pltpu.VMEM((128, 3 * D), bf16), pltpu.VMEM((128, D), bf16)),
        in_specs=[vmem, hbm],
        out_specs=(vmem, vmem),
        scratch_shapes=[pltpu.VMEM((D, 3 * D), bf16), pltpu.SemaphoreType.DMA],
        compiler_params=pltpu.CompilerParams(vmem_limit_bytes=VMEM_LIMIT),
        name="tables",
    )(codebook, off_chip(qkv_weight))

    scalars = [
        pltpu.SMEM((down * across, qr * qc, lanes), i32),
        pltpu.SMEM(logit_scale.shape, f32),
    ]
    n1 = geo.r1n * geo.c1n * AREA
    nh = geo.half * geo.c0n * AREA
    cout = conv_weight.shape[3]
    own, wq1, wo1, wc = pl.pallas_call(
        functools.partial(first_body, geo),
        out_shape=(
            pltpu.VMEM((nh, D), bf16),
            pltpu.VMEM((D, 3 * D), bf16),
            pltpu.VMEM((D, D), bf16),
            pltpu.VMEM((3, 3, D, cout), bf16),
        ),
        in_specs=[hbm, vmem, vmem, vmem, hbm, hbm, hbm],
        out_specs=(vmem,) * 4,
        scratch_shapes=[
            *scalars,
            pltpu.VMEM((n1, 128), bf16),
            pltpu.VMEM((n1, 1), f32),
            pltpu.VMEM((n1, D), bf16),
            pltpu.VMEM((nh, D), bf16),
            pltpu.VMEM((n1, D), bf16),
            pltpu.VMEM((n1, D), bf16),
            pltpu.VMEM((nh, D), bf16),
            pltpu.VMEM((D, D), bf16),
            pltpu.SemaphoreType.DMA((6,)),
        ],
        compiler_params=pltpu.CompilerParams(vmem_limit_bytes=VMEM_LIMIT),
        name="first",
    )(
        off_chip(logit_scale), on_chip(everyone), on_chip(table), on_chip(padded),
        *map(off_chip, (qkv_weight, out_weight, conv_weight)),
    )
    other = own
    if geo.sides == 2:
        other = lax.ppermute(own, "ha", [(n, n ^ 1) for n in range(down)])

    n0 = geo.r0n * geo.c0n * AREA
    nq = qr * (qc + 2) * AREA + 2 * (qc + 2) * STRIP
    window = pltpu.VMEM((n0, D), bf16)
    wq1, wo1, wc = map(on_chip, (wq1, wo1, wc))
    state = pl.pallas_call(
        functools.partial(own_keys_body, geo),
        out_shape=(window,) * 3,
        in_specs=[vmem, vmem],
        out_specs=(vmem,) * 3,
        compiler_params=pltpu.CompilerParams(vmem_limit_bytes=VMEM_LIMIT),
        name="own_keys",
    )(on_chip(own), wq1)
    return pl.pallas_call(
        functools.partial(second_body, geo),
        out_shape=(jax.ShapeDtypeStruct((qr * TILE, qc * TILE, cout), bf16),) + (window,) * 3,
        in_specs=[hbm] + [vmem] * 8,
        out_specs=(vmem,) * 4,
        input_output_aliases={6: 1, 7: 2, 8: 3},
        scratch_shapes=[
            *scalars,
            pltpu.VMEM((nq, D), bf16),
            pltpu.VMEM((nq, D), bf16),
            pltpu.VMEM((nq, D), bf16),
            pltpu.VMEM((qr * TILE + 2, (qc + 2) * TILE, D), f32),
            pltpu.SemaphoreType.DMA((2,)),
        ],
        compiler_params=pltpu.CompilerParams(vmem_limit_bytes=VMEM_LIMIT),
        name="second",
    )(
        off_chip(logit_scale), on_chip(everyone), on_chip(other), wq1, wo1, wc,
        *map(on_chip, state),
    )[0]


def solution(mesh):
    in_specs = (
        P(("parts", "ha", "wa"), None),
        P(("parts", "ha"), "wa", None),
        P(),
        P(),
        P(),
        P(),
        P(),
    )
    out_specs = P(("parts", "ha"), "wa", None)
    return jax.shard_map(local, mesh=mesh, in_specs=in_specs, out_specs=out_specs, check_vma=False)
```

```python
import functools
import math

import jax
import jax.numpy as jnp
from jax import lax
from jax.experimental import pallas as pl
from jax.experimental.pallas import tpu as pltpu
from jax.sharding import PartitionSpec as P

D = 512
HEADS = 8
HEAD = D // HEADS
TILE = 8
AREA = TILE * TILE
NSEL = 6
BLOCKS = 2
HALF = 256
GROUP = HALF // HEAD
digit_levels = (8, 8, 8, 5, 5, 5)
digit_shift = (6, 3, 0, 9, 12, 15)
norm_eps = 1e-06
LOG2E = math.log2(math.e)
NEG = -1e30

f32 = jnp.float32
bf16 = jnp.bfloat16
i32 = jnp.int32


def mm(a, b):
    return lax.dot_general(a, b, (((1,), (0,)), ((), ())), preferred_element_type=f32)


def mm_t(a, b):
    return lax.dot_general(a, b, (((1,), (1,)), ((), ())), preferred_element_type=f32)


def span(count, size, total):
    return jnp.clip(count, 0, total - size)


def reach(starts, size, total):
    return max(min(s + size + 1, total) - max(s - 1, 0) for s in starts)


def pack_digits(ids):
    x = ids.astype(f32)
    q5 = jnp.floor((x + 0.5) * 0.2)
    q4 = jnp.floor((q5 + 0.5) * 0.2)
    q3 = jnp.floor((q4 + 0.5) * 0.2)
    return q3 + 512.0 * (q4 - 5.0 * q3) + 4096.0 * (q5 - 5.0 * q4) + 32768.0 * (x - 5.0 * q5)


def slot_tables():
    lane = lax.broadcasted_iota(i32, (1, 128), 1)
    slot = lane & 63
    shift = jnp.zeros_like(lane)
    start = jnp.zeros_like(lane)
    offset = 0
    for size, bits in zip(digit_levels, digit_shift):
        here = slot >= offset
        shift = jnp.where(here, bits, shift)
        start = jnp.where(here, offset, start)
        offset += size
    return shift, jnp.where(slot < offset, slot - start, -1)


def head_scale(x, ones_bd, floor):
    parts = []
    for half in range(D // HALF):
        piece = x[:, HALF * half : HALF * half + HALF]
        total = mm((piece * piece).astype(bf16), ones_bd)
        parts.append((piece * lax.rsqrt(total * (1.0 / HEAD) + floor)).astype(bf16))
    return jnp.concatenate(parts, axis=1)


def square_mean(x):
    return jnp.sum(x * x, axis=-1, keepdims=True) * (1.0 / D)


def attend_tile(q, starts, bias, factors, keys, values, lane_head):
    outs = []
    for g in range(D // HALF):
        cols = slice(HALF * g, HALF * g + HALF)
        qg = q[:, cols]
        q_bd = jnp.concatenate(
            [jnp.where(lane_head == h, qg, jnp.zeros_like(qg)) for h in range(GROUP)], axis=0
        )
        k = jnp.concatenate([keys[pl.ds(s, AREA), cols] for s in starts], axis=0)
        v = jnp.concatenate([values[pl.ds(s, AREA), cols] for s in starts], axis=0)
        s = mm_t(q_bd, k) + bias
        s = s - jnp.max(s, axis=-1, keepdims=True)
        p = jnp.concatenate(
            [
                jnp.exp2(s[AREA * h : AREA * h + AREA] * factors[GROUP * g + h])
                for h in range(GROUP)
            ],
            axis=0,
        )
        den = jnp.sum(p, axis=-1, keepdims=True)
        o = mm(p.astype(bf16), v) * (1.0 / den)
        r = o[:AREA]
        for h in range(1, GROUP):
            r = jnp.where(lane_head == h, o[AREA * h : AREA * h + AREA], r)
        outs.append(r)
    return jnp.concatenate(outs, axis=1).astype(bf16)


def attend_strip(q, starts, bias, factors, keys, values):
    count = q.shape[0]
    lane_head = lax.broadcasted_iota(i32, (1, D), 1) // HEAD
    q_bd = jnp.concatenate(
        [jnp.where(lane_head == h, q, jnp.zeros_like(q)) for h in range(HEADS)], axis=0
    )
    k = jnp.concatenate([keys[pl.ds(s, AREA), :] for s in starts], axis=0)
    v = jnp.concatenate([values[pl.ds(s, AREA), :] for s in starts], axis=0)
    s = mm_t(q_bd, k) + bias
    s = s - jnp.max(s, axis=-1, keepdims=True)
    p = jnp.concatenate(
        [jnp.exp2(s[count * h : count * h + count] * factors[h]) for h in range(HEADS)], axis=0
    )
    den = jnp.sum(p, axis=-1, keepdims=True)
    o = mm(p.astype(bf16), v) * (1.0 / den)
    r = o[:count]
    for h in range(1, HEADS):
        r = jnp.where(lane_head == h, o[count * h : count * h + count], r)
    return r.astype(bf16)


def block_ones():
    return (
        lax.broadcasted_iota(i32, (HALF, HALF), 0) // HEAD
        == lax.broadcasted_iota(i32, (HALF, HALF), 1) // HEAD
    ).astype(f32).astype(bf16)


def factors_of(scale_ref, layer):
    return [scale_ref[layer, h] * (LOG2E / math.sqrt(HEAD)) for h in range(HEADS)]


def rows_at(tile, count=AREA):
    return pl.ds(pl.multiple_of(tile * AREA, AREA), count)


def neighbours(geo, lists_ref, gi, gj, row0, col0, cols):
    gi = jnp.clip(gi, 0, geo.tr - 1)
    gj = jnp.clip(gj, 0, geo.tc - 1)
    owner = gi // geo.qr * (geo.tc // geo.qc) + gj // geo.qc
    at = gi % geo.qr * geo.qc + gj % geo.qc
    bias_tile = lax.broadcasted_iota(i32, (1, NSEL * AREA), 1) // AREA
    starts = []
    bias = jnp.zeros((1, NSEL * AREA), f32)
    for n in range(NSEL):
        number = lists_ref[owner, at, n]
        ni = gi - 1 + number // 3
        nj = gj - 1 + number % 3
        inside = (ni >= 0) & (ni < geo.tr) & (nj >= 0) & (nj < geo.tc)
        ni = jnp.where(inside, ni, gi)
        nj = jnp.where(inside, nj, gj)
        starts.append(pl.multiple_of(((ni - row0) * cols + nj - col0) * AREA, AREA))
        bias = jnp.where(bias_tile == n, jnp.where(inside, 0.0, NEG), bias)
    return starts, bias


class Geometry:
    def __init__(self, rr, width, qr, qc, down, across):
        self.rr, self.width, self.qr, self.qc = rr, width, qr, qc
        self.tr, self.tc = qr * down, qc * across
        self.sides = 2 if down % 2 == 0 else 1
        pair = qr * self.sides
        self.r0n = min(pair + 4, self.tr)
        if self.r0n % self.sides:
            self.sides, pair = 1, qr
            self.r0n = min(pair + 4, self.tr)
        self.pair = pair
        self.half = self.r0n // self.sides
        self.c0n = min(qc + 4, self.tc)
        clip = lambda at, size, total: min(max(at, 0), total - size)
        self.c1n = reach(
            [clip(n * qc - 2, self.c0n, self.tc) for n in range(across)], self.c0n, self.tc
        )
        self.r1n = reach(
            [
                clip(n * pair - 2, self.r0n, self.tr) + side * self.half
                for n in range(self.tr // pair)
                for side in range(self.sides)
            ],
            self.half,
            self.tr,
        )

    def place(self):
        ha, wa = lax.axis_index("ha"), lax.axis_index("wa")
        own_r, own_c = ha * self.qr, wa * self.qc
        side = ha % self.sides
        p0 = span(ha // self.sides * self.pair - 2, self.r0n, self.tr)
        c0 = span(own_c - 2, self.c0n, self.tc)
        r0 = p0 + side * self.half
        r1 = span(r0 - 1, self.r1n, self.tr)
        c1 = span(c0 - 1, self.c1n, self.tc)
        return own_r, own_c, side, p0, r0, c0, r1, c1


def first_body(
    geo,
    scale_hbm, ids_ref, table_ref, book_ref, wq_hbm, wo_hbm, wc_hbm,
    out_ref, wq1_ref, wo1_ref, wc_ref,
    lists_ref, scale_ref, onehot, floors, hid0, q0, k0, v0, att, wo, sems,
):
    copies = [
        pltpu.make_async_copy(ids_ref.at[:, pl.ds(geo.rr, geo.qr * geo.qc), :], lists_ref, sems.at[0]),
        pltpu.make_async_copy(scale_hbm, scale_ref, sems.at[1]),
        pltpu.make_async_copy(wo_hbm.at[0], wo, sems.at[2]),
        pltpu.make_async_copy(wq_hbm.at[1], wq1_ref, sems.at[3]),
        pltpu.make_async_copy(wo_hbm.at[1], wo1_ref, sems.at[4]),
        pltpu.make_async_copy(wc_hbm, wc_ref, sems.at[5]),
    ]
    for copy in copies:
        copy.start()
    own_r, own_c, side, p0, r0, c0, r1, c1 = geo.place()
    c0n, c1n, rr = geo.c0n, geo.c1n, geo.rr
    lane_head = lax.broadcasted_iota(i32, (1, HALF), 1) // HEAD
    ones_bd = block_ones()

    shift, digit = slot_tables()
    lanes = ids_ref.shape[2]
    rel = (
        lax.broadcasted_iota(i32, (AREA, lanes), 1)
        - lax.broadcasted_iota(i32, (AREA, lanes), 0) % TILE
    )
    per_tile = TILE // rr
    for i in range(geo.r1n):
        rows = []
        for n in range(per_tile):
            packed = pack_digits(ids_ref[(r1 + i) * per_tile + n])
            rows += [jnp.broadcast_to(packed[r : r + 1], (TILE, lanes)) for r in range(rr)]
        spread = jnp.concatenate(rows, axis=0)
        for j in range(c1n):
            mine = jnp.where(rel == TILE * (c1 + j), spread, 0.0)
            code = jnp.sum(mine, axis=-1, keepdims=True).astype(i32)
            hit = (lax.shift_right_logical(jnp.broadcast_to(code, (AREA, 128)), shift) & 7) == digit
            t = i * c1n + j
            onehot[AREA * t : AREA * t + AREA, :] = hit.astype(f32).astype(bf16)

    def project_keys(i, _):
        rows = rows_at(i * c1n, c1n * AREA)
        oh = onehot[rows, :]
        hid = mm(oh, book_ref[...]).astype(bf16)
        hid0[rows, :] = hid
        ms = square_mean(hid.astype(f32)) + norm_eps
        floor = norm_eps * ms
        floors[rows, :] = floor
        k0[rows, :] = head_scale(mm(oh, table_ref[:, D : 2 * D]), ones_bd, floor)
        v0[rows, :] = (mm(oh, table_ref[:, 2 * D :]) * lax.rsqrt(ms)).astype(bf16)
        return 0

    for i in range(geo.r1n):
        project_keys(i, 0)

    def in_window(i):
        return rows_at((r0 - r1 + i) * c1n + c0 - c1, c0n * AREA)

    def project_queries(i, _):
        rows = in_window(i)
        q = mm(onehot[rows, :], table_ref[:, :D])
        q0[rows_at(i * c0n, c0n * AREA), :] = head_scale(q, ones_bd, floors[rows, :])
        return 0

    for i in range(geo.half):
        project_queries(i, 0)

    copies[0].wait()
    copies[1].wait()
    factors = factors_of(scale_ref, 0)

    def attend(i, _):
        for j in range(c0n):
            starts, bias = neighbours(geo, lists_ref, r0 + i, c0 + j, r1, c1, c1n)
            here = rows_at(i * c0n + j)
            att[here, :] = attend_tile(q0[here, :], starts, bias, factors, k0, v0, lane_head)
        return 0

    for i in range(geo.half):
        attend(i, 0)

    copies[2].wait()

    def project_out(i, _):
        rows = rows_at(i * c0n, c0n * AREA)
        old = hid0[in_window(i), :].astype(f32)
        out_ref[rows, :] = (old + mm(att[rows, :], wo[...])).astype(bf16)
        return 0

    for i in range(geo.half):
        project_out(i, 0)
    for copy in copies[3:]:
        copy.wait()


def layer1_keys(hid, wq, ones_bd, rows, k1, v1):
    h = hid[rows, :]
    ms = square_mean(h.astype(f32)) + norm_eps
    k1[rows, :] = head_scale(mm(h, wq[:, D : 2 * D]), ones_bd, norm_eps * ms)
    v1[rows, :] = (mm(h, wq[:, 2 * D :]) * lax.rsqrt(ms)).astype(bf16)


def half_keys(geo, source, side, wq, hid, k1, v1, unroll):
    ones_bd = block_ones()
    step = geo.c0n
    first = side * geo.half

    def one(i, _):
        rows = rows_at((first + i) * step, step * AREA)
        hid[rows, :] = source[rows_at(i * step, step * AREA), :]
        layer1_keys(hid, wq, ones_bd, rows, k1, v1)
        return 0

    if unroll:
        for i in range(geo.half):
            one(i, 0)
    else:
        lax.fori_loop(0, geo.half, one, 0)


def own_keys_body(geo, own_ref, wq, hid, k1, v1):
    side = geo.place()[2]
    half_keys(geo, own_ref, side, wq, hid, k1, v1, True)


STRIP = 16


def second_body(
    geo,
    scale_hbm, ids_ref, other_ref, wq, wo, wc, hid_in, k1_in, v1_in,
    out_ref, hid, k1, v1,
    lists_ref, scale_ref, queries, q1, att, region, sems,
):
    copies = [
        pltpu.make_async_copy(ids_ref.at[:, pl.ds(geo.rr, geo.qr * geo.qc), :], lists_ref, sems.at[0]),
        pltpu.make_async_copy(scale_hbm, scale_ref, sems.at[1]),
    ]
    for copy in copies:
        copy.start()
    own_r, own_c, side, p0, r0, c0, r1, c1 = geo.place()
    c0n, qr, qc = geo.c0n, geo.qr, geo.qc
    lane_head = lax.broadcasted_iota(i32, (1, HALF), 1) // HEAD
    ones_bd = block_ones()
    if geo.sides == 2:
        half_keys(geo, other_ref, 1 - side, wq, hid, k1, v1, False)

    ring = qc + 2

    def clipped(gi, gj):
        ci = jnp.clip(gi, 0, geo.tr - 1)
        cj = jnp.clip(gj, 0, geo.tc - 1)
        return (ci - p0) * c0n + cj - c0

    whole = [(own_r + i, own_c - 1 + j) for i in range(qr) for j in range(ring)]
    strips = [(own_r - 1, own_c - 1 + j, AREA - STRIP) for j in range(ring)]
    strips += [(own_r + qr, own_c - 1 + j, 0) for j in range(ring)]
    base = len(whole) * AREA
    for n, (gi, gj) in enumerate(whole):
        queries[AREA * n : AREA * n + AREA, :] = hid[rows_at(clipped(gi, gj)), :]
    for n, (gi, gj, skip) in enumerate(strips):
        at = base + STRIP * n
        here = pl.ds(pl.multiple_of(clipped(gi, gj) * AREA + skip, STRIP), STRIP)
        queries[at : at + STRIP, :] = hid[here, :]
    h = queries[...]
    ms = square_mean(h.astype(f32)) + norm_eps
    q1[...] = head_scale(mm(h, wq[:, :D]), ones_bd, norm_eps * ms)

    for copy in copies:
        copy.wait()
    factors = factors_of(scale_ref, 1)
    for n, (gi, gj) in enumerate(whole):
        starts, bias = neighbours(geo, lists_ref, gi, gj, p0, c0, c0n)
        at = slice(AREA * n, AREA * n + AREA)
        att[at, :] = attend_tile(q1[at, :], starts, bias, factors, k1, v1, lane_head)
    for n, (gi, gj, _) in enumerate(strips):
        starts, bias = neighbours(geo, lists_ref, gi, gj, p0, c0, c0n)
        at = slice(base + STRIP * n, base + STRIP * n + STRIP)
        att[at, :] = attend_strip(q1[at, :], starts, bias, factors, k1, v1)

    h = (queries[...].astype(f32) + mm(att[...], wo[...])).astype(bf16).astype(f32)
    v = h * lax.rsqrt(square_mean(h) + norm_eps)
    act = v / (1.0 + jnp.exp(-v))

    def kept(piece, gi, gj):
        inside = (gi >= 0) & (gi < geo.tr) & (gj >= 0) & (gj < geo.tc)
        return jnp.where(inside, piece, 0.0)

    for n, (gi, gj) in enumerate(whole):
        i, j = divmod(n, ring)
        tile = kept(act[AREA * n : AREA * n + AREA], gi, gj)
        for r in range(TILE):
            region[1 + TILE * i + r, TILE * j : TILE * j + TILE, :] = tile[TILE * r : TILE * r + TILE]
    for n, (gi, gj, skip) in enumerate(strips):
        i, j = divmod(n, ring)
        at = base + STRIP * n + (STRIP - TILE if skip else 0)
        row = (qr * TILE + 1) * i
        region[row, TILE * j : TILE * j + TILE, :] = kept(act[at : at + TILE], gi, gj)

    rows, cols = qr * TILE, qc * TILE
    total = jnp.zeros((rows * cols, wc.shape[-1]), f32)
    for dc in range(3):
        left = TILE - 1 + dc
        shifted = region[:, left : left + cols, :].astype(bf16)
        for dr in range(3):
            piece = shifted[dr : dr + rows].reshape(rows * cols, D)
            total = total + mm(piece, wc[dr, dc])
    out_ref[...] = total.astype(bf16).reshape(rows, cols, wc.shape[-1])


def table_body(book_ref, wq_hbm, table_ref, padded_ref, wq, sem):
    copy = pltpu.make_async_copy(wq_hbm.at[0], wq, sem)
    copy.start()
    book = jnp.concatenate(
        [book_ref[...].astype(f32), jnp.zeros((64 - book_ref.shape[0], D), f32)], axis=0
    ).astype(bf16)
    copy.wait()
    full = mm(book, wq[...])
    high = full.astype(bf16)
    low = (full - high.astype(f32)).astype(bf16)
    table_ref[...] = jnp.concatenate([high, low], axis=0)
    padded_ref[...] = jnp.concatenate([book, jnp.zeros_like(book)], axis=0)


VMEM_LIMIT = 20 << 20


def on_chip(x):
    return pltpu.with_memory_space_constraint(x, pltpu.VMEM)


def off_chip(x):
    return pltpu.with_memory_space_constraint(x, pltpu.HBM)


vmem = pl.BlockSpec(memory_space=pltpu.VMEM)
hbm = pl.BlockSpec(memory_space=pltpu.HBM)


def local(token_ids, neighbour_lists, codebook, qkv_weight, out_weight, logit_scale, conv_weight):
    across = lax.axis_size("wa")
    down = lax.axis_size("ha")
    rr, width = token_ids.shape
    qr, qc = neighbour_lists.shape[:2]
    assert TILE % rr == 0
    geo = Geometry(rr, width, qr, qc, down, across)
    lists = neighbour_lists.reshape(qr * qc, NSEL)
    lanes = -(-width // 128) * 128
    group = down * across
    count = rr + qr * qc
    mine = jnp.pad(
        jnp.broadcast_to(token_ids, (group, rr, width)), ((0, 0), (0, count - rr), (0, lanes - width))
    ) + jnp.pad(
        jnp.broadcast_to(lists, (group, qr * qc, NSEL)), ((0, 0), (rr, 0), (0, lanes - NSEL))
    )
    everyone = lax.all_to_all(mine, ("ha", "wa"), 0, 0, tiled=True)

    table, padded = pl.pallas_call(
        table_body,
        out_shape=(pltpu.VMEM((128, 3 * D), bf16), pltpu.VMEM((128, D), bf16)),
        in_specs=[vmem, hbm],
        out_specs=(vmem, vmem),
        scratch_shapes=[pltpu.VMEM((D, 3 * D), bf16), pltpu.SemaphoreType.DMA],
        compiler_params=pltpu.CompilerParams(vmem_limit_bytes=VMEM_LIMIT),
        name="tables",
    )(codebook, off_chip(qkv_weight))

    scalars = [
        pltpu.SMEM((down * across, qr * qc, lanes), i32),
        pltpu.SMEM(logit_scale.shape, f32),
    ]
    n1 = geo.r1n * geo.c1n * AREA
    nh = geo.half * geo.c0n * AREA
    cout = conv_weight.shape[3]
    own, wq1, wo1, wc = pl.pallas_call(
        functools.partial(first_body, geo),
        out_shape=(
            pltpu.VMEM((nh, D), bf16),
            pltpu.VMEM((D, 3 * D), bf16),
            pltpu.VMEM((D, D), bf16),
            pltpu.VMEM((3, 3, D, cout), bf16),
        ),
        in_specs=[hbm, vmem, vmem, vmem, hbm, hbm, hbm],
        out_specs=(vmem,) * 4,
        scratch_shapes=[
            *scalars,
            pltpu.VMEM((n1, 128), bf16),
            pltpu.VMEM((n1, 1), f32),
            pltpu.VMEM((n1, D), bf16),
            pltpu.VMEM((nh, D), bf16),
            pltpu.VMEM((n1, D), bf16),
            pltpu.VMEM((n1, D), bf16),
            pltpu.VMEM((nh, D), bf16),
            pltpu.VMEM((D, D), bf16),
            pltpu.SemaphoreType.DMA((6,)),
        ],
        compiler_params=pltpu.CompilerParams(vmem_limit_bytes=VMEM_LIMIT),
        name="first",
    )(
        off_chip(logit_scale), on_chip(everyone), on_chip(table), on_chip(padded),
        *map(off_chip, (qkv_weight, out_weight, conv_weight)),
    )
    other = own
    if geo.sides == 2:
        other = lax.ppermute(own, "ha", [(n, n ^ 1) for n in range(down)])

    n0 = geo.r0n * geo.c0n * AREA
    nq = qr * (qc + 2) * AREA + 2 * (qc + 2) * STRIP
    window = pltpu.VMEM((n0, D), bf16)
    wq1, wo1, wc = map(on_chip, (wq1, wo1, wc))
    state = pl.pallas_call(
        functools.partial(own_keys_body, geo),
        out_shape=(window,) * 3,
        in_specs=[vmem, vmem],
        out_specs=(vmem,) * 3,
        compiler_params=pltpu.CompilerParams(vmem_limit_bytes=VMEM_LIMIT),
        name="own_keys",
    )(on_chip(own), wq1)
    return pl.pallas_call(
        functools.partial(second_body, geo),
        out_shape=(jax.ShapeDtypeStruct((qr * TILE, qc * TILE, cout), bf16),) + (window,) * 3,
        in_specs=[hbm] + [vmem] * 8,
        out_specs=(vmem,) * 4,
        input_output_aliases={6: 1, 7: 2, 8: 3},
        scratch_shapes=[
            *scalars,
            pltpu.VMEM((nq, D), bf16),
            pltpu.VMEM((nq, D), bf16),
            pltpu.VMEM((nq, D), bf16),
            pltpu.VMEM((qr * TILE + 2, (qc + 2) * TILE, D), f32),
            pltpu.SemaphoreType.DMA((2,)),
        ],
        compiler_params=pltpu.CompilerParams(vmem_limit_bytes=VMEM_LIMIT),
        name="second",
    )(
        off_chip(logit_scale), on_chip(everyone), on_chip(other), wq1, wo1, wc,
        *map(on_chip, state),
    )[0]


def solution(mesh):
    in_specs = (
        P(("parts", "ha", "wa"), None),
        P(("parts", "ha"), "wa", None),
        P(),
        P(),
        P(),
        P(),
        P(),
    )
    out_specs = P(("parts", "ha"), "wa", None)
    return jax.shard_map(local, mesh=mesh, in_specs=in_specs, out_specs=out_specs, check_vma=False)
```

```python
import functools
import math

import jax
import jax.numpy as jnp
from jax import lax
from jax.experimental import pallas as pl
from jax.experimental.pallas import tpu as pltpu
from jax.sharding import PartitionSpec as P

D = 512
HEADS = 8
HEAD = D // HEADS
TILE = 8
AREA = TILE * TILE
NSEL = 6
BLOCKS = 2
HALF = 256
GROUP = HALF // HEAD
digit_levels = (8, 8, 8, 5, 5, 5)
digit_shift = (6, 3, 0, 9, 12, 15)
norm_eps = 1e-06
LOG2E = math.log2(math.e)
NEG = -1e30

f32 = jnp.float32
bf16 = jnp.bfloat16
i32 = jnp.int32


def mm(a, b):
    return lax.dot_general(a, b, (((1,), (0,)), ((), ())), preferred_element_type=f32)


def mm_t(a, b):
    return lax.dot_general(a, b, (((1,), (1,)), ((), ())), preferred_element_type=f32)


def span(count, size, total):
    return jnp.clip(count, 0, total - size)


def reach(starts, size, total):
    return max(min(s + size + 1, total) - max(s - 1, 0) for s in starts)


def pack_digits(ids):
    x = ids.astype(f32)
    q5 = jnp.floor((x + 0.5) * 0.2)
    q4 = jnp.floor((q5 + 0.5) * 0.2)
    q3 = jnp.floor((q4 + 0.5) * 0.2)
    return q3 + 512.0 * (q4 - 5.0 * q3) + 4096.0 * (q5 - 5.0 * q4) + 32768.0 * (x - 5.0 * q5)


def slot_tables():
    lane = lax.broadcasted_iota(i32, (1, 128), 1)
    slot = lane & 63
    shift = jnp.zeros_like(lane)
    start = jnp.zeros_like(lane)
    offset = 0
    for size, bits in zip(digit_levels, digit_shift):
        here = slot >= offset
        shift = jnp.where(here, bits, shift)
        start = jnp.where(here, offset, start)
        offset += size
    return shift, jnp.where(slot < offset, slot - start, -1)


def head_scale(x, ones_bd, floor):
    parts = []
    for half in range(D // HALF):
        piece = x[:, HALF * half : HALF * half + HALF]
        total = mm((piece * piece).astype(bf16), ones_bd)
        parts.append((piece * lax.rsqrt(total * (1.0 / HEAD) + floor)).astype(bf16))
    return jnp.concatenate(parts, axis=1)


def square_mean(x):
    return jnp.sum(x * x, axis=-1, keepdims=True) * (1.0 / D)


def attend_tile(q, starts, bias, factors, keys, values, lane_head):
    outs = []
    for g in range(D // HALF):
        cols = slice(HALF * g, HALF * g + HALF)
        qg = q[:, cols]
        q_bd = jnp.concatenate(
            [jnp.where(lane_head == h, qg, jnp.zeros_like(qg)) for h in range(GROUP)], axis=0
        )
        k = jnp.concatenate([keys[pl.ds(s, AREA), cols] for s in starts], axis=0)
        v = jnp.concatenate([values[pl.ds(s, AREA), cols] for s in starts], axis=0)
        s = mm_t(q_bd, k) + bias
        s = s - jnp.max(s, axis=-1, keepdims=True)
        p = jnp.concatenate(
            [
                jnp.exp2(s[AREA * h : AREA * h + AREA] * factors[GROUP * g + h])
                for h in range(GROUP)
            ],
            axis=0,
        )
        den = jnp.sum(p, axis=-1, keepdims=True)
        o = mm(p.astype(bf16), v) * (1.0 / den)
        r = o[:AREA]
        for h in range(1, GROUP):
            r = jnp.where(lane_head == h, o[AREA * h : AREA * h + AREA], r)
        outs.append(r)
    return jnp.concatenate(outs, axis=1).astype(bf16)


def attend_strip(q, starts, bias, factors, keys, values):
    count = q.shape[0]
    lane_head = lax.broadcasted_iota(i32, (1, D), 1) // HEAD
    q_bd = jnp.concatenate(
        [jnp.where(lane_head == h, q, jnp.zeros_like(q)) for h in range(HEADS)], axis=0
    )
    k = jnp.concatenate([keys[pl.ds(s, AREA), :] for s in starts], axis=0)
    v = jnp.concatenate([values[pl.ds(s, AREA), :] for s in starts], axis=0)
    s = mm_t(q_bd, k) + bias
    s = s - jnp.max(s, axis=-1, keepdims=True)
    p = jnp.concatenate(
        [jnp.exp2(s[count * h : count * h + count] * factors[h]) for h in range(HEADS)], axis=0
    )
    den = jnp.sum(p, axis=-1, keepdims=True)
    o = mm(p.astype(bf16), v) * (1.0 / den)
    r = o[:count]
    for h in range(1, HEADS):
        r = jnp.where(lane_head == h, o[count * h : count * h + count], r)
    return r.astype(bf16)


def block_ones():
    return (
        lax.broadcasted_iota(i32, (HALF, HALF), 0) // HEAD
        == lax.broadcasted_iota(i32, (HALF, HALF), 1) // HEAD
    ).astype(f32).astype(bf16)


def factors_of(scale_ref, layer):
    return [scale_ref[layer, h] * (LOG2E / math.sqrt(HEAD)) for h in range(HEADS)]


def rows_at(tile, count=AREA):
    return pl.ds(pl.multiple_of(tile * AREA, AREA), count)


def neighbours(geo, lists_ref, gi, gj, row0, col0, cols, skipped=0):
    gi = jnp.clip(gi, 0, geo.tr - 1)
    gj = jnp.clip(gj, 0, geo.tc - 1)
    owner = gi // geo.qr * (geo.tc // geo.qc) + gj // geo.qc - skipped
    at = gi % geo.qr * geo.qc + gj % geo.qc
    bias_tile = lax.broadcasted_iota(i32, (1, NSEL * AREA), 1) // AREA
    starts = []
    bias = jnp.zeros((1, NSEL * AREA), f32)
    for n in range(NSEL):
        number = lists_ref[owner, at, n]
        ni = gi - 1 + number // 3
        nj = gj - 1 + number % 3
        inside = (ni >= 0) & (ni < geo.tr) & (nj >= 0) & (nj < geo.tc)
        ni = jnp.where(inside, ni, gi)
        nj = jnp.where(inside, nj, gj)
        starts.append(pl.multiple_of(((ni - row0) * cols + nj - col0) * AREA, AREA))
        bias = jnp.where(bias_tile == n, jnp.where(inside, 0.0, NEG), bias)
    return starts, bias


class Geometry:
    def __init__(self, rr, width, qr, qc, down, across):
        self.rr, self.width, self.qr, self.qc = rr, width, qr, qc
        self.tr, self.tc = qr * down, qc * across
        self.sides = 2 if down % 2 == 0 else 1
        pair = qr * self.sides
        self.r0n = min(pair + 4, self.tr)
        if self.r0n % self.sides:
            self.sides, pair = 1, qr
            self.r0n = min(pair + 4, self.tr)
        self.pair = pair
        self.half = self.r0n // self.sides
        self.c0n = min(qc + 4, self.tc)
        clip = lambda at, size, total: min(max(at, 0), total - size)
        self.c1n = reach(
            [clip(n * qc - 2, self.c0n, self.tc) for n in range(across)], self.c0n, self.tc
        )
        self.r1n = reach(
            [
                clip(n * pair - 2, self.r0n, self.tr) + side * self.half
                for n in range(self.tr // pair)
                for side in range(self.sides)
            ],
            self.half,
            self.tr,
        )

    def place(self):
        ha, wa = lax.axis_index("ha"), lax.axis_index("wa")
        own_r, own_c = ha * self.qr, wa * self.qc
        side = ha % self.sides
        p0 = span(ha // self.sides * self.pair - 2, self.r0n, self.tr)
        c0 = span(own_c - 2, self.c0n, self.tc)
        r0 = p0 + side * self.half
        r1 = span(r0 - 1, self.r1n, self.tr)
        c1 = span(c0 - 1, self.c1n, self.tc)
        return own_r, own_c, side, p0, r0, c0, r1, c1


def first_body(
    geo,
    scale_hbm, ids_ref, table_ref, book_ref, wq_hbm, wo_hbm, wc_hbm,
    out_ref, wq1_ref, wo1_ref, wc_ref,
    lists_ref, scale_ref, onehot, floors, hid0, q0, k0, v0, att, wo, sems,
):
    copies = [
        pltpu.make_async_copy(ids_ref.at[:, pl.ds(geo.rr, geo.qr * geo.qc), :], lists_ref, sems.at[0]),
        pltpu.make_async_copy(scale_hbm, scale_ref, sems.at[1]),
        pltpu.make_async_copy(wo_hbm.at[0], wo, sems.at[2]),
        pltpu.make_async_copy(wq_hbm.at[1], wq1_ref, sems.at[3]),
        pltpu.make_async_copy(wo_hbm.at[1], wo1_ref, sems.at[4]),
        pltpu.make_async_copy(wc_hbm, wc_ref, sems.at[5]),
    ]
    for copy in copies:
        copy.start()
    own_r, own_c, side, p0, r0, c0, r1, c1 = geo.place()
    c0n, c1n, rr = geo.c0n, geo.c1n, geo.rr
    lane_head = lax.broadcasted_iota(i32, (1, HALF), 1) // HEAD
    ones_bd = block_ones()

    shift, digit = slot_tables()
    lanes = ids_ref.shape[2]
    rel = (
        lax.broadcasted_iota(i32, (AREA, lanes), 1)
        - lax.broadcasted_iota(i32, (AREA, lanes), 0) % TILE
    )
    per_tile = TILE // rr
    for i in range(geo.r1n):
        rows = []
        for n in range(per_tile):
            packed = pack_digits(ids_ref[(r1 + i) * per_tile + n])
            rows += [jnp.broadcast_to(packed[r : r + 1], (TILE, lanes)) for r in range(rr)]
        spread = jnp.concatenate(rows, axis=0)
        for j in range(c1n):
            mine = jnp.where(rel == TILE * (c1 + j), spread, 0.0)
            code = jnp.sum(mine, axis=-1, keepdims=True).astype(i32)
            hit = (lax.shift_right_logical(jnp.broadcast_to(code, (AREA, 128)), shift) & 7) == digit
            t = i * c1n + j
            onehot[AREA * t : AREA * t + AREA, :] = hit.astype(f32).astype(bf16)

    def project_keys(i, _):
        rows = rows_at(i * c1n, c1n * AREA)
        oh = onehot[rows, :]
        hid = mm(oh, book_ref[...]).astype(bf16)
        hid0[rows, :] = hid
        ms = square_mean(hid.astype(f32)) + norm_eps
        floor = norm_eps * ms
        floors[rows, :] = floor
        k0[rows, :] = head_scale(mm(oh, table_ref[:, D : 2 * D]), ones_bd, floor)
        v0[rows, :] = (mm(oh, table_ref[:, 2 * D :]) * lax.rsqrt(ms)).astype(bf16)
        return 0

    for i in range(geo.r1n):
        project_keys(i, 0)

    def in_window(i):
        return rows_at((r0 - r1 + i) * c1n + c0 - c1, c0n * AREA)

    def project_queries(i, _):
        rows = in_window(i)
        q = mm(onehot[rows, :], table_ref[:, :D])
        q0[rows_at(i * c0n, c0n * AREA), :] = head_scale(q, ones_bd, floors[rows, :])
        return 0

    for i in range(geo.half):
        project_queries(i, 0)

    copies[0].wait()
    copies[1].wait()
    factors = factors_of(scale_ref, 0)

    def attend(i, _):
        for j in range(c0n):
            starts, bias = neighbours(geo, lists_ref, r0 + i, c0 + j, r1, c1, c1n)
            here = rows_at(i * c0n + j)
            att[here, :] = attend_tile(q0[here, :], starts, bias, factors, k0, v0, lane_head)
        return 0

    for i in range(geo.half):
        attend(i, 0)

    copies[2].wait()

    def project_out(i, _):
        rows = rows_at(i * c0n, c0n * AREA)
        old = hid0[in_window(i), :].astype(f32)
        out_ref[rows, :] = (old + mm(att[rows, :], wo[...])).astype(bf16)
        return 0

    for i in range(geo.half):
        project_out(i, 0)
    for copy in copies[3:]:
        copy.wait()


def layer1_keys(hid, wq, ones_bd, rows, k1, v1):
    h = hid[rows, :]
    ms = square_mean(h.astype(f32)) + norm_eps
    k1[rows, :] = head_scale(mm(h, wq[:, D : 2 * D]), ones_bd, norm_eps * ms)
    v1[rows, :] = (mm(h, wq[:, 2 * D :]) * lax.rsqrt(ms)).astype(bf16)


def half_keys(geo, source, side, wq, hid, k1, v1, unroll):
    ones_bd = block_ones()
    step = geo.c0n
    first = side * geo.half

    def one(i, _):
        rows = rows_at((first + i) * step, step * AREA)
        hid[rows, :] = source[rows_at(i * step, step * AREA), :]
        layer1_keys(hid, wq, ones_bd, rows, k1, v1)
        return 0

    if unroll:
        for i in range(geo.half):
            one(i, 0)
    else:
        lax.fori_loop(0, geo.half, one, 0)


def own_keys_body(geo, own_ref, wq, hid, k1, v1):
    side = geo.place()[2]
    half_keys(geo, own_ref, side, wq, hid, k1, v1, True)


STRIP = 16
EARLY = 2


def finish(queries, attended, wo, inside):
    h = (queries.astype(f32) + mm(attended, wo)).astype(bf16).astype(f32)
    v = h * lax.rsqrt(square_mean(h) + norm_eps)
    act = v / (1.0 + jnp.exp(-v))
    share = act.shape[0] // len(inside)
    return [
        jnp.where(flag, act[share * n : share * n + share], 0.0) for n, flag in enumerate(inside)
    ]


def on_grid(geo, gi, gj):
    return (gi >= 0) & (gi < geo.tr) & (gj >= 0) & (gj < geo.tc)


def strip_tiles(geo, own_r, own_c, side):
    above = (own_r - 1, AREA - STRIP)
    below = (own_r + geo.qr, 0)
    if geo.sides == 2:
        edges = [tuple(jnp.where(side == 0, x, y) for x, y in zip(above, below))]
    else:
        edges = [above, below]
    return [(gi, own_c - 1 + j, skip) for gi, skip in edges for j in range(geo.qc + 2)]


def rows_body(
    geo,
    scale_hbm, ids_ref, other_ref, wq, wo, hid_in, k1_in, v1_in,
    middle, edge, queries_out, q1_out, early, hid, k1, v1,
    lists_ref, scale_ref, queries, q1, att, sems,
):
    copies = [
        pltpu.make_async_copy(ids_ref.at[:, pl.ds(geo.rr, geo.qr * geo.qc), :], lists_ref, sems.at[0]),
        pltpu.make_async_copy(scale_hbm, scale_ref, sems.at[1]),
    ]
    for copy in copies:
        copy.start()
    own_r, own_c, side, p0, r0, c0, r1, c1 = geo.place()
    c0n, qr, qc = geo.c0n, geo.qr, geo.qc
    lane_head = lax.broadcasted_iota(i32, (1, HALF), 1) // HEAD
    ones_bd = block_ones()
    if geo.sides == 2:
        half_keys(geo, other_ref, 1 - side, wq, hid, k1, v1, False)

    ring = qc + 2

    def clipped(gi, gj):
        ci = jnp.clip(gi, 0, geo.tr - 1)
        cj = jnp.clip(gj, 0, geo.tc - 1)
        return (ci - p0) * c0n + cj - c0

    whole = [(own_r + i, own_c - 1 + j) for i in range(qr) for j in range(ring)]
    strips = strip_tiles(geo, own_r, own_c, side)
    base = len(whole) * AREA
    for n, (gi, gj) in enumerate(whole):
        queries[AREA * n : AREA * n + AREA, :] = hid[rows_at(clipped(gi, gj)), :]
    for n, (gi, gj, skip) in enumerate(strips):
        at = base + STRIP * n
        here = pl.ds(pl.multiple_of(clipped(gi, gj) * AREA + skip, STRIP), STRIP)
        queries[at : at + STRIP, :] = hid[here, :]
    h = queries[...]
    ms = square_mean(h.astype(f32)) + norm_eps
    q = head_scale(mm(h, wq[:, :D]), ones_bd, norm_eps * ms)
    q1[...] = q[:base]
    q1_out[...] = q[base:]
    queries_out[...] = h[base:]

    for copy in copies:
        copy.wait()
    factors = factors_of(scale_ref, 1)
    for n, (gi, gj) in enumerate(whole):
        starts, bias = neighbours(geo, lists_ref, gi, gj, p0, c0, c0n)
        at = slice(AREA * n, AREA * n + AREA)
        att[at, :] = attend_tile(q1[at, :], starts, bias, factors, k1, v1, lane_head)
    for n, (gi, gj, _) in enumerate(strips[:EARLY]):
        starts, bias = neighbours(geo, lists_ref, gi, gj, p0, c0, c0n)
        at = slice(STRIP * n, STRIP * n + STRIP)
        early[at, :] = attend_strip(q[base:][at], starts, bias, factors, k1, v1)

    done = finish(
        queries[:base, :], att[...], wo[...], [on_grid(geo, gi, gj) for gi, gj in whole]
    )
    for n, tile in enumerate(done):
        i, j = divmod(n, ring)
        for r in range(TILE):
            middle[TILE * i + r, TILE * j : TILE * j + TILE, :] = tile[TILE * r : TILE * r + TILE]
    for j in range(ring):
        last = done[(qr - 1) * ring + j][AREA - TILE :]
        edge[TILE * j : TILE * j + TILE, :] = jnp.where(side == 0, last, done[j][:TILE]).astype(bf16)


def rim_body(
    geo,
    scale_vmem, ids_ref, queries, q1, early, k1, v1, wo,
    outer,
    lists_ref, scale_ref, att, sems,
):
    own_r, own_c, side, p0, r0, c0, r1, c1 = geo.place()
    strips = strip_tiles(geo, own_r, own_c, side)
    owners = lists_ref.shape[0]
    skipped = 0
    if geo.sides == 2:
        skipped = jnp.clip(strips[0][0], 0, geo.tr - 1) // geo.qr * owners
    copies = [
        pltpu.make_async_copy(
            ids_ref.at[pl.ds(skipped, owners), pl.ds(geo.rr, geo.qr * geo.qc), :],
            lists_ref,
            sems.at[0],
        ),
        pltpu.make_async_copy(scale_vmem, scale_ref, sems.at[1]),
    ]
    for copy in copies:
        copy.start()
    for copy in copies:
        copy.wait()
    factors = factors_of(scale_ref, 1)
    att[: STRIP * EARLY, :] = early[...]
    for n, (gi, gj, _) in enumerate(strips):
        if n < EARLY:
            continue
        starts, bias = neighbours(geo, lists_ref, gi, gj, p0, c0, geo.c0n, skipped)
        at = slice(STRIP * n, STRIP * n + STRIP)
        att[at, :] = attend_strip(q1[at, :], starts, bias, factors, k1, v1)
    done = finish(
        queries[...], att[...], wo[...], [on_grid(geo, gi, gj) for gi, gj, _ in strips]
    )
    for n, (strip, (_, _, skip)) in enumerate(zip(done, strips)):
        row = jnp.where(skip > 0, strip[STRIP - TILE :], strip[:TILE])
        outer[TILE * n : TILE * n + TILE, :] = row.astype(bf16)


def conv_body(geo, middle, outer, received, wc, out_ref, region):
    rows, cols = geo.qr * TILE, geo.qc * TILE
    side = geo.place()[2]
    wide = (geo.qc + 2) * TILE
    first = outer[:wide, :].astype(f32)
    second = (received if geo.sides == 2 else outer)[-wide:, :].astype(f32)
    if geo.sides == 2:
        first, second = jnp.where(side == 0, first, second), jnp.where(side == 0, second, first)
    region[0] = first
    region[1] = second
    total = jnp.zeros((rows * cols, wc.shape[-1]), f32)
    for dc in range(3):
        left = TILE - 1 + dc
        inner = middle[:, left : left + cols, :].astype(bf16)
        rims = region[:, left : left + cols, :].astype(bf16)
        shifted = jnp.concatenate([rims[:1], inner, rims[1:]], axis=0)
        for dr in range(3):
            piece = shifted[dr : dr + rows].reshape(rows * cols, D)
            total = total + mm(piece, wc[dr, dc])
    out_ref[...] = total.astype(bf16).reshape(rows, cols, wc.shape[-1])


def table_body(book_ref, wq_hbm, table_ref, padded_ref, wq, sem):
    copy = pltpu.make_async_copy(wq_hbm.at[0], wq, sem)
    copy.start()
    book = jnp.concatenate(
        [book_ref[...].astype(f32), jnp.zeros((64 - book_ref.shape[0], D), f32)], axis=0
    ).astype(bf16)
    copy.wait()
    full = mm(book, wq[...])
    high = full.astype(bf16)
    low = (full - high.astype(f32)).astype(bf16)
    table_ref[...] = jnp.concatenate([high, low], axis=0)
    padded_ref[...] = jnp.concatenate([book, jnp.zeros_like(book)], axis=0)


VMEM_LIMIT = 20 << 20


def on_chip(x):
    return pltpu.with_memory_space_constraint(x, pltpu.VMEM)


def off_chip(x):
    return pltpu.with_memory_space_constraint(x, pltpu.HBM)


vmem = pl.BlockSpec(memory_space=pltpu.VMEM)
hbm = pl.BlockSpec(memory_space=pltpu.HBM)


def local(token_ids, neighbour_lists, codebook, qkv_weight, out_weight, logit_scale, conv_weight):
    across = lax.axis_size("wa")
    down = lax.axis_size("ha")
    rr, width = token_ids.shape
    qr, qc = neighbour_lists.shape[:2]
    assert TILE % rr == 0
    geo = Geometry(rr, width, qr, qc, down, across)
    lists = neighbour_lists.reshape(qr * qc, NSEL)
    lanes = -(-width // 128) * 128
    group = down * across
    count = rr + qr * qc
    mine = jnp.pad(
        jnp.broadcast_to(token_ids, (group, rr, width)), ((0, 0), (0, count - rr), (0, lanes - width))
    ) + jnp.pad(
        jnp.broadcast_to(lists, (group, qr * qc, NSEL)), ((0, 0), (rr, 0), (0, lanes - NSEL))
    )
    everyone = lax.all_to_all(mine, ("ha", "wa"), 0, 0, tiled=True)

    table, padded = pl.pallas_call(
        table_body,
        out_shape=(pltpu.VMEM((128, 3 * D), bf16), pltpu.VMEM((128, D), bf16)),
        in_specs=[vmem, hbm],
        out_specs=(vmem, vmem),
        scratch_shapes=[pltpu.VMEM((D, 3 * D), bf16), pltpu.SemaphoreType.DMA],
        compiler_params=pltpu.CompilerParams(vmem_limit_bytes=VMEM_LIMIT),
        name="tables",
    )(codebook, off_chip(qkv_weight))

    scalars = [
        pltpu.SMEM((down * across, qr * qc, lanes), i32),
        pltpu.SMEM(logit_scale.shape, f32),
    ]
    n1 = geo.r1n * geo.c1n * AREA
    nh = geo.half * geo.c0n * AREA
    cout = conv_weight.shape[3]
    own, wq1, wo1, wc = pl.pallas_call(
        functools.partial(first_body, geo),
        out_shape=(
            pltpu.VMEM((nh, D), bf16),
            pltpu.VMEM((D, 3 * D), bf16),
            pltpu.VMEM((D, D), bf16),
            pltpu.VMEM((3, 3, D, cout), bf16),
        ),
        in_specs=[hbm, vmem, vmem, vmem, hbm, hbm, hbm],
        out_specs=(vmem,) * 4,
        scratch_shapes=[
            *scalars,
            pltpu.VMEM((n1, 128), bf16),
            pltpu.VMEM((n1, 1), f32),
            pltpu.VMEM((n1, D), bf16),
            pltpu.VMEM((nh, D), bf16),
            pltpu.VMEM((n1, D), bf16),
            pltpu.VMEM((n1, D), bf16),
            pltpu.VMEM((nh, D), bf16),
            pltpu.VMEM((D, D), bf16),
            pltpu.SemaphoreType.DMA((6,)),
        ],
        compiler_params=pltpu.CompilerParams(vmem_limit_bytes=VMEM_LIMIT),
        name="first",
    )(
        off_chip(logit_scale), on_chip(everyone), on_chip(table), on_chip(padded),
        *map(off_chip, (qkv_weight, out_weight, conv_weight)),
    )
    other = own
    if geo.sides == 2:
        other = lax.ppermute(own, "ha", [(n, n ^ 1) for n in range(down)])

    n0 = geo.r0n * geo.c0n * AREA
    ring = qc + 2
    whole = qr * ring * AREA
    strips = ring * STRIP * (3 - geo.sides)
    window = pltpu.VMEM((n0, D), bf16)
    wq1, wo1, wc = map(on_chip, (wq1, wo1, wc))
    limit = pltpu.CompilerParams(vmem_limit_bytes=VMEM_LIMIT)
    scale, everyone = off_chip(logit_scale), on_chip(everyone)
    state = pl.pallas_call(
        functools.partial(own_keys_body, geo),
        out_shape=(window,) * 3,
        in_specs=[vmem, vmem],
        out_specs=(vmem,) * 3,
        compiler_params=limit,
        name="own_keys",
    )(on_chip(own), wq1)
    middle, edge, queries, q1, early, _, k1, v1 = pl.pallas_call(
        functools.partial(rows_body, geo),
        out_shape=(
            pltpu.VMEM((qr * TILE, ring * TILE, D), f32),
            pltpu.VMEM((ring * TILE, D), bf16),
            pltpu.VMEM((strips, D), bf16),
            pltpu.VMEM((strips, D), bf16),
            pltpu.VMEM((STRIP * EARLY, D), bf16),
        )
        + (window,) * 3,
        in_specs=[hbm] + [vmem] * 7,
        out_specs=(vmem,) * 8,
        input_output_aliases={5: 5, 6: 6, 7: 7},
        scratch_shapes=[
            *scalars,
            pltpu.VMEM((whole + strips, D), bf16),
            pltpu.VMEM((whole, D), bf16),
            pltpu.VMEM((whole, D), bf16),
            pltpu.SemaphoreType.DMA((2,)),
        ],
        compiler_params=limit,
        name="rows",
    )(scale, everyone, on_chip(other), wq1, wo1, *map(on_chip, state))
    received = edge
    if geo.sides == 2:
        received = lax.ppermute(edge, "ha", [(n, n ^ 1) for n in range(down)])
    outer = pl.pallas_call(
        functools.partial(rim_body, geo),
        out_shape=pltpu.VMEM((ring * TILE * (3 - geo.sides), D), bf16),
        in_specs=[vmem] * 8,
        out_specs=vmem,
        scratch_shapes=[
            pltpu.SMEM((across if geo.sides == 2 else down * across, qr * qc, lanes), i32),
            scalars[1],
            pltpu.VMEM((strips, D), bf16),
            pltpu.SemaphoreType.DMA((2,)),
        ],
        compiler_params=limit,
        name="rim",
    )(on_chip(logit_scale), everyone, *map(on_chip, (queries, q1, early, k1, v1)), wo1)
    return pl.pallas_call(
        functools.partial(conv_body, geo),
        out_shape=jax.ShapeDtypeStruct((qr * TILE, qc * TILE, cout), bf16),
        in_specs=[vmem] * 4,
        out_specs=vmem,
        scratch_shapes=[pltpu.VMEM((2, ring * TILE, D), f32)],
        compiler_params=limit,
        name="conv",
    )(*map(on_chip, (middle, outer, received)), wc)


def solution(mesh):
    in_specs = (
        P(("parts", "ha", "wa"), None),
        P(("parts", "ha"), "wa", None),
        P(),
        P(),
        P(),
        P(),
        P(),
    )
    out_specs = P(("parts", "ha"), "wa", None)
    return jax.shard_map(local, mesh=mesh, in_specs=in_specs, out_specs=out_specs, check_vma=False)
```

```python
import functools
import math

import jax
import jax.numpy as jnp
from jax import lax
from jax.experimental import pallas as pl
from jax.experimental.pallas import tpu as pltpu
from jax.sharding import PartitionSpec as P

D = 512
HEADS = 8
HEAD = D // HEADS
TILE = 8
AREA = TILE * TILE
NSEL = 6
BLOCKS = 2
HALF = 256
GROUP = HALF // HEAD
digit_levels = (8, 8, 8, 5, 5, 5)
digit_shift = (6, 3, 0, 9, 12, 15)
norm_eps = 1e-06
LOG2E = math.log2(math.e)
NEG = -1e30

f32 = jnp.float32
bf16 = jnp.bfloat16
i32 = jnp.int32


def mm(a, b):
    return lax.dot_general(a, b, (((1,), (0,)), ((), ())), preferred_element_type=f32)


def mm_t(a, b):
    return lax.dot_general(a, b, (((1,), (1,)), ((), ())), preferred_element_type=f32)


def span(count, size, total):
    return jnp.clip(count, 0, total - size)


def reach(starts, size, total):
    return max(min(s + size + 1, total) - max(s - 1, 0) for s in starts)


def pack_digits(ids):
    x = ids.astype(f32)
    q5 = jnp.floor((x + 0.5) * 0.2)
    q4 = jnp.floor((q5 + 0.5) * 0.2)
    q3 = jnp.floor((q4 + 0.5) * 0.2)
    return q3 + 512.0 * (q4 - 5.0 * q3) + 4096.0 * (q5 - 5.0 * q4) + 32768.0 * (x - 5.0 * q5)


def slot_tables():
    lane = lax.broadcasted_iota(i32, (1, 128), 1)
    slot = lane & 63
    shift = jnp.zeros_like(lane)
    start = jnp.zeros_like(lane)
    offset = 0
    for size, bits in zip(digit_levels, digit_shift):
        here = slot >= offset
        shift = jnp.where(here, bits, shift)
        start = jnp.where(here, offset, start)
        offset += size
    return shift, jnp.where(slot < offset, slot - start, -1)


def head_scale(x, ones_bd, floor):
    parts = []
    for half in range(D // HALF):
        piece = x[:, HALF * half : HALF * half + HALF]
        total = mm((piece * piece).astype(bf16), ones_bd)
        parts.append((piece * lax.rsqrt(total * (1.0 / HEAD) + floor)).astype(bf16))
    return jnp.concatenate(parts, axis=1)


def square_mean(x):
    return jnp.sum(x * x, axis=-1, keepdims=True) * (1.0 / D)


def attend_tile(q, starts, bias, factors, keys, values, lane_head):
    outs = []
    for g in range(D // HALF):
        cols = slice(HALF * g, HALF * g + HALF)
        qg = q[:, cols]
        q_bd = jnp.concatenate(
            [jnp.where(lane_head == h, qg, jnp.zeros_like(qg)) for h in range(GROUP)], axis=0
        )
        k = jnp.concatenate([keys[pl.ds(s, AREA), cols] for s in starts], axis=0)
        v = jnp.concatenate([values[pl.ds(s, AREA), cols] for s in starts], axis=0)
        s = mm_t(q_bd, k) + bias
        s = s - jnp.max(s, axis=-1, keepdims=True)
        p = jnp.concatenate(
            [
                jnp.exp2(s[AREA * h : AREA * h + AREA] * factors[GROUP * g + h])
                for h in range(GROUP)
            ],
            axis=0,
        )
        den = jnp.sum(p, axis=-1, keepdims=True)
        o = mm(p.astype(bf16), v) * (1.0 / den)
        r = o[:AREA]
        for h in range(1, GROUP):
            r = jnp.where(lane_head == h, o[AREA * h : AREA * h + AREA], r)
        outs.append(r)
    return jnp.concatenate(outs, axis=1).astype(bf16)


def attend_strip(q, starts, bias, factors, keys, values):
    count = q.shape[0]
    lane_head = lax.broadcasted_iota(i32, (1, D), 1) // HEAD
    q_bd = jnp.concatenate(
        [jnp.where(lane_head == h, q, jnp.zeros_like(q)) for h in range(HEADS)], axis=0
    )
    k = jnp.concatenate([keys[pl.ds(s, AREA), :] for s in starts], axis=0)
    v = jnp.concatenate([values[pl.ds(s, AREA), :] for s in starts], axis=0)
    s = mm_t(q_bd, k) + bias
    s = s - jnp.max(s, axis=-1, keepdims=True)
    p = jnp.concatenate(
        [jnp.exp2(s[count * h : count * h + count] * factors[h]) for h in range(HEADS)], axis=0
    )
    den = jnp.sum(p, axis=-1, keepdims=True)
    o = mm(p.astype(bf16), v) * (1.0 / den)
    r = o[:count]
    for h in range(1, HEADS):
        r = jnp.where(lane_head == h, o[count * h : count * h + count], r)
    return r.astype(bf16)


def block_ones():
    return (
        lax.broadcasted_iota(i32, (HALF, HALF), 0) // HEAD
        == lax.broadcasted_iota(i32, (HALF, HALF), 1) // HEAD
    ).astype(f32).astype(bf16)


def factors_of(scale_ref, layer):
    return [scale_ref[layer, h] * (LOG2E / math.sqrt(HEAD)) for h in range(HEADS)]


def rows_at(tile, count=AREA):
    return pl.ds(pl.multiple_of(tile * AREA, AREA), count)


def neighbours(geo, lists_ref, gi, gj, row0, col0, cols, skipped=0):
    gi = jnp.clip(gi, 0, geo.tr - 1)
    gj = jnp.clip(gj, 0, geo.tc - 1)
    owner = gi // geo.qr * (geo.tc // geo.qc) + gj // geo.qc - skipped
    at = gi % geo.qr * geo.qc + gj % geo.qc
    bias_tile = lax.broadcasted_iota(i32, (1, NSEL * AREA), 1) // AREA
    starts = []
    bias = jnp.zeros((1, NSEL * AREA), f32)
    for n in range(NSEL):
        number = lists_ref[owner, at, n]
        ni = gi - 1 + number // 3
        nj = gj - 1 + number % 3
        inside = (ni >= 0) & (ni < geo.tr) & (nj >= 0) & (nj < geo.tc)
        ni = jnp.where(inside, ni, gi)
        nj = jnp.where(inside, nj, gj)
        starts.append(pl.multiple_of(((ni - row0) * cols + nj - col0) * AREA, AREA))
        bias = jnp.where(bias_tile == n, jnp.where(inside, 0.0, NEG), bias)
    return starts, bias


class Geometry:
    def __init__(self, rr, width, qr, qc, down, across):
        self.rr, self.width, self.qr, self.qc = rr, width, qr, qc
        self.tr, self.tc = qr * down, qc * across
        self.sides = 2 if down % 2 == 0 else 1
        pair = qr * self.sides
        self.r0n = min(pair + 4, self.tr)
        if self.r0n % self.sides:
            self.sides, pair = 1, qr
            self.r0n = min(pair + 4, self.tr)
        self.pair = pair
        self.half = self.r0n // self.sides
        self.c0n = min(qc + 4, self.tc)
        clip = lambda at, size, total: min(max(at, 0), total - size)
        self.c1n = reach(
            [clip(n * qc - 2, self.c0n, self.tc) for n in range(across)], self.c0n, self.tc
        )
        self.r1n = reach(
            [
                clip(n * pair - 2, self.r0n, self.tr) + side * self.half
                for n in range(self.tr // pair)
                for side in range(self.sides)
            ],
            self.half,
            self.tr,
        )

    def place(self):
        ha, wa = lax.axis_index("ha"), lax.axis_index("wa")
        own_r, own_c = ha * self.qr, wa * self.qc
        side = ha % self.sides
        p0 = span(ha // self.sides * self.pair - 2, self.r0n, self.tr)
        c0 = span(own_c - 2, self.c0n, self.tc)
        r0 = p0 + side * self.half
        r1 = span(r0 - 1, self.r1n, self.tr)
        c1 = span(c0 - 1, self.c1n, self.tc)
        return own_r, own_c, side, p0, r0, c0, r1, c1


def first_body(
    geo,
    scale_hbm, ids_ref, table_ref, book_ref, wq_hbm, wo_hbm, wc_hbm,
    out_ref, wq1_ref, wo1_ref, wc_ref,
    lists_ref, scale_ref, onehot, floors, hid0, q0, k0, v0, att, wo, sems,
):
    copies = [
        pltpu.make_async_copy(ids_ref.at[:, pl.ds(geo.rr, geo.qr * geo.qc), :], lists_ref, sems.at[0]),
        pltpu.make_async_copy(scale_hbm, scale_ref, sems.at[1]),
        pltpu.make_async_copy(wo_hbm.at[0], wo, sems.at[2]),
        pltpu.make_async_copy(wq_hbm.at[1], wq1_ref, sems.at[3]),
        pltpu.make_async_copy(wo_hbm.at[1], wo1_ref, sems.at[4]),
        pltpu.make_async_copy(wc_hbm, wc_ref, sems.at[5]),
    ]
    for copy in copies:
        copy.start()
    own_r, own_c, side, p0, r0, c0, r1, c1 = geo.place()
    c0n, c1n, rr = geo.c0n, geo.c1n, geo.rr
    lane_head = lax.broadcasted_iota(i32, (1, HALF), 1) // HEAD
    ones_bd = block_ones()

    shift, digit = slot_tables()
    lanes = ids_ref.shape[2]
    rel = (
        lax.broadcasted_iota(i32, (AREA, lanes), 1)
        - lax.broadcasted_iota(i32, (AREA, lanes), 0) % TILE
    )
    per_tile = TILE // rr
    for i in range(geo.r1n):
        rows = []
        for n in range(per_tile):
            packed = pack_digits(ids_ref[(r1 + i) * per_tile + n])
            rows += [jnp.broadcast_to(packed[r : r + 1], (TILE, lanes)) for r in range(rr)]
        spread = jnp.concatenate(rows, axis=0)
        for j in range(c1n):
            mine = jnp.where(rel == TILE * (c1 + j), spread, 0.0)
            code = jnp.sum(mine, axis=-1, keepdims=True).astype(i32)
            hit = (lax.shift_right_logical(jnp.broadcast_to(code, (AREA, 128)), shift) & 7) == digit
            t = i * c1n + j
            onehot[AREA * t : AREA * t + AREA, :] = hit.astype(f32).astype(bf16)

    def project_keys(i, _):
        rows = rows_at(i * c1n, c1n * AREA)
        oh = onehot[rows, :]
        hid = mm(oh, book_ref[...]).astype(bf16)
        hid0[rows, :] = hid
        ms = square_mean(hid.astype(f32)) + norm_eps
        floor = norm_eps * ms
        floors[rows, :] = floor
        k0[rows, :] = head_scale(mm(oh, table_ref[:, D : 2 * D]), ones_bd, floor)
        v0[rows, :] = (mm(oh, table_ref[:, 2 * D :]) * lax.rsqrt(ms)).astype(bf16)
        return 0

    for i in range(geo.r1n):
        project_keys(i, 0)

    def in_window(i):
        return rows_at((r0 - r1 + i) * c1n + c0 - c1, c0n * AREA)

    def project_queries(i, _):
        rows = in_window(i)
        q = mm(onehot[rows, :], table_ref[:, :D])
        q0[rows_at(i * c0n, c0n * AREA), :] = head_scale(q, ones_bd, floors[rows, :])
        return 0

    for i in range(geo.half):
        project_queries(i, 0)

    copies[0].wait()
    copies[1].wait()
    factors = factors_of(scale_ref, 0)

    def attend(i, _):
        for j in range(c0n):
            starts, bias = neighbours(geo, lists_ref, r0 + i, c0 + j, r1, c1, c1n)
            here = rows_at(i * c0n + j)
            att[here, :] = attend_tile(q0[here, :], starts, bias, factors, k0, v0, lane_head)
        return 0

    for i in range(geo.half):
        attend(i, 0)

    copies[2].wait()

    def project_out(i, _):
        rows = rows_at(i * c0n, c0n * AREA)
        old = hid0[in_window(i), :].astype(f32)
        out_ref[rows, :] = (old + mm(att[rows, :], wo[...])).astype(bf16)
        return 0

    for i in range(geo.half):
        project_out(i, 0)
    for copy in copies[3:]:
        copy.wait()


def layer1_keys(hid, wq, ones_bd, rows, k1, v1):
    h = hid[rows, :]
    ms = square_mean(h.astype(f32)) + norm_eps
    k1[rows, :] = head_scale(mm(h, wq[:, D : 2 * D]), ones_bd, norm_eps * ms)
    v1[rows, :] = (mm(h, wq[:, 2 * D :]) * lax.rsqrt(ms)).astype(bf16)


def half_keys(geo, source, side, wq, hid, k1, v1, unroll):
    ones_bd = block_ones()
    step = geo.c0n
    first = side * geo.half

    def one(i, _):
        rows = rows_at((first + i) * step, step * AREA)
        hid[rows, :] = source[rows_at(i * step, step * AREA), :]
        layer1_keys(hid, wq, ones_bd, rows, k1, v1)
        return 0

    if unroll:
        for i in range(geo.half):
            one(i, 0)
    else:
        lax.fori_loop(0, geo.half, one, 0)


def own_keys_body(geo, own_ref, wq, hid, k1, v1):
    side = geo.place()[2]
    half_keys(geo, own_ref, side, wq, hid, k1, v1, True)


STRIP = 16


def finish(queries, attended, wo, inside):
    h = (queries.astype(f32) + mm(attended, wo)).astype(bf16).astype(f32)
    v = h * lax.rsqrt(square_mean(h) + norm_eps)
    act = v / (1.0 + jnp.exp(-v))
    share = act.shape[0] // len(inside)
    return [
        jnp.where(flag, act[share * n : share * n + share], 0.0) for n, flag in enumerate(inside)
    ]


def on_grid(geo, gi, gj):
    return (gi >= 0) & (gi < geo.tr) & (gj >= 0) & (gj < geo.tc)


def strip_tiles(geo, own_r, own_c, side):
    above = (own_r - 1, AREA - STRIP)
    below = (own_r + geo.qr, 0)
    if geo.sides == 2:
        edges = [tuple(jnp.where(side == 0, x, y) for x, y in zip(above, below))]
    else:
        edges = [above, below]
    return [(gi, own_c - 1 + j, skip) for gi, skip in edges for j in range(geo.qc + 2)]


def rows_body(
    geo,
    scale_hbm, ids_ref, other_ref, wq, wo, hid_in, k1_in, v1_in,
    edge, queries, att, hid, k1, v1,
    lists_ref, scale_ref, q1, sems,
):
    copies = [
        pltpu.make_async_copy(ids_ref.at[:, pl.ds(geo.rr, geo.qr * geo.qc), :], lists_ref, sems.at[0]),
        pltpu.make_async_copy(scale_hbm, scale_ref, sems.at[1]),
    ]
    for copy in copies:
        copy.start()
    own_r, own_c, side, p0, r0, c0, r1, c1 = geo.place()
    c0n, qr, qc = geo.c0n, geo.qr, geo.qc
    lane_head = lax.broadcasted_iota(i32, (1, HALF), 1) // HEAD
    ones_bd = block_ones()
    if geo.sides == 2:
        half_keys(geo, other_ref, 1 - side, wq, hid, k1, v1, False)

    ring = qc + 2

    def clipped(gi, gj):
        ci = jnp.clip(gi, 0, geo.tr - 1)
        cj = jnp.clip(gj, 0, geo.tc - 1)
        return (ci - p0) * c0n + cj - c0

    whole = [(own_r + i, own_c - 1 + j) for i in range(qr) for j in range(ring)]
    strips = strip_tiles(geo, own_r, own_c, side)
    base = len(whole) * AREA
    for n, (gi, gj) in enumerate(whole):
        queries[AREA * n : AREA * n + AREA, :] = hid[rows_at(clipped(gi, gj)), :]
    for n, (gi, gj, skip) in enumerate(strips):
        at = base + STRIP * n
        here = pl.ds(pl.multiple_of(clipped(gi, gj) * AREA + skip, STRIP), STRIP)
        queries[at : at + STRIP, :] = hid[here, :]
    h = queries[...]
    ms = square_mean(h.astype(f32)) + norm_eps
    q = head_scale(mm(h, wq[:, :D]), ones_bd, norm_eps * ms)
    q1[...] = q

    for copy in copies:
        copy.wait()
    factors = factors_of(scale_ref, 1)
    for n, (gi, gj) in enumerate(whole):
        starts, bias = neighbours(geo, lists_ref, gi, gj, p0, c0, c0n)
        at = slice(AREA * n, AREA * n + AREA)
        att[at, :] = attend_tile(q1[at, :], starts, bias, factors, k1, v1, lane_head)
    for n, (gi, gj, _) in enumerate(strips):
        starts, bias = neighbours(geo, lists_ref, gi, gj, p0, c0, c0n)
        at = slice(base + STRIP * n, base + STRIP * n + STRIP)
        att[at, :] = attend_strip(q1[at, :], starts, bias, factors, k1, v1)

    picked = [
        pl.ds(
            pl.multiple_of(
                jnp.where(side == 0, ((qr - 1) * ring + j) * AREA + AREA - STRIP, j * AREA), STRIP
            ),
            STRIP,
        )
        for j in range(ring)
    ]
    done = finish(
        jnp.concatenate([queries[at, :] for at in picked], axis=0),
        jnp.concatenate([att[at, :] for at in picked], axis=0),
        wo[...],
        [on_grid(geo, own_r, own_c - 1 + j) for j in range(ring)],
    )
    for j, strip in enumerate(done):
        row = jnp.where(side == 0, strip[STRIP - TILE :], strip[:TILE])
        edge[TILE * j : TILE * j + TILE, :] = row.astype(bf16)


def finish_body(geo, queries, att, wo, middle, outer):
    own_r, own_c, side = geo.place()[:3]
    qr, ring = geo.qr, geo.qc + 2
    whole = [(own_r + i, own_c - 1 + j) for i in range(qr) for j in range(ring)]
    strips = strip_tiles(geo, own_r, own_c, side)
    base = len(whole) * AREA
    flags = [on_grid(geo, gi, gj) for gi, gj in whole for _ in range(AREA // STRIP)]
    flags += [on_grid(geo, gi, gj) for gi, gj, _ in strips]
    done = finish(queries[...], att[...], wo[...], flags)
    for n, piece in enumerate(done[: base // STRIP]):
        i, j = divmod(n // (AREA // STRIP), ring)
        row = TILE * i + n % (AREA // STRIP) * (STRIP // TILE)
        for r in range(STRIP // TILE):
            middle[row + r, TILE * j : TILE * j + TILE, :] = piece[TILE * r : TILE * r + TILE]
    for n, (strip, (_, _, skip)) in enumerate(zip(done[base // STRIP :], strips)):
        row = jnp.where(skip > 0, strip[STRIP - TILE :], strip[:TILE])
        outer[TILE * n : TILE * n + TILE, :] = row.astype(bf16)


def conv_body(geo, middle, outer, received, wc, out_ref, region):
    rows, cols = geo.qr * TILE, geo.qc * TILE
    side = geo.place()[2]
    wide = (geo.qc + 2) * TILE
    first = outer[:wide, :].astype(f32)
    second = (received if geo.sides == 2 else outer)[-wide:, :].astype(f32)
    if geo.sides == 2:
        first, second = jnp.where(side == 0, first, second), jnp.where(side == 0, second, first)
    region[0] = first
    region[1] = second
    total = jnp.zeros((rows * cols, wc.shape[-1]), f32)
    for dc in range(3):
        left = TILE - 1 + dc
        inner = middle[:, left : left + cols, :].astype(bf16)
        rims = region[:, left : left + cols, :].astype(bf16)
        shifted = jnp.concatenate([rims[:1], inner, rims[1:]], axis=0)
        for dr in range(3):
            piece = shifted[dr : dr + rows].reshape(rows * cols, D)
            total = total + mm(piece, wc[dr, dc])
    out_ref[...] = total.astype(bf16).reshape(rows, cols, wc.shape[-1])


def table_body(book_ref, wq_hbm, table_ref, padded_ref, wq, sem):
    copy = pltpu.make_async_copy(wq_hbm.at[0], wq, sem)
    copy.start()
    book = jnp.concatenate(
        [book_ref[...].astype(f32), jnp.zeros((64 - book_ref.shape[0], D), f32)], axis=0
    ).astype(bf16)
    copy.wait()
    full = mm(book, wq[...])
    high = full.astype(bf16)
    low = (full - high.astype(f32)).astype(bf16)
    table_ref[...] = jnp.concatenate([high, low], axis=0)
    padded_ref[...] = jnp.concatenate([book, jnp.zeros_like(book)], axis=0)


VMEM_LIMIT = 20 << 20


def on_chip(x):
    return pltpu.with_memory_space_constraint(x, pltpu.VMEM)


def off_chip(x):
    return pltpu.with_memory_space_constraint(x, pltpu.HBM)


vmem = pl.BlockSpec(memory_space=pltpu.VMEM)
hbm = pl.BlockSpec(memory_space=pltpu.HBM)


def local(token_ids, neighbour_lists, codebook, qkv_weight, out_weight, logit_scale, conv_weight):
    across = lax.axis_size("wa")
    down = lax.axis_size("ha")
    rr, width = token_ids.shape
    qr, qc = neighbour_lists.shape[:2]
    assert TILE % rr == 0
    geo = Geometry(rr, width, qr, qc, down, across)
    lists = neighbour_lists.reshape(qr * qc, NSEL)
    lanes = -(-width // 128) * 128
    group = down * across
    count = rr + qr * qc
    mine = jnp.pad(
        jnp.broadcast_to(token_ids, (group, rr, width)), ((0, 0), (0, count - rr), (0, lanes - width))
    ) + jnp.pad(
        jnp.broadcast_to(lists, (group, qr * qc, NSEL)), ((0, 0), (rr, 0), (0, lanes - NSEL))
    )
    everyone = lax.all_to_all(mine, ("ha", "wa"), 0, 0, tiled=True)

    table, padded = pl.pallas_call(
        table_body,
        out_shape=(pltpu.VMEM((128, 3 * D), bf16), pltpu.VMEM((128, D), bf16)),
        in_specs=[vmem, hbm],
        out_specs=(vmem, vmem),
        scratch_shapes=[pltpu.VMEM((D, 3 * D), bf16), pltpu.SemaphoreType.DMA],
        compiler_params=pltpu.CompilerParams(vmem_limit_bytes=VMEM_LIMIT),
        name="tables",
    )(codebook, off_chip(qkv_weight))

    scalars = [
        pltpu.SMEM((down * across, qr * qc, lanes), i32),
        pltpu.SMEM(logit_scale.shape, f32),
    ]
    n1 = geo.r1n * geo.c1n * AREA
    nh = geo.half * geo.c0n * AREA
    cout = conv_weight.shape[3]
    own, wq1, wo1, wc = pl.pallas_call(
        functools.partial(first_body, geo),
        out_shape=(
            pltpu.VMEM((nh, D), bf16),
            pltpu.VMEM((D, 3 * D), bf16),
            pltpu.VMEM((D, D), bf16),
            pltpu.VMEM((3, 3, D, cout), bf16),
        ),
        in_specs=[hbm, vmem, vmem, vmem, hbm, hbm, hbm],
        out_specs=(vmem,) * 4,
        scratch_shapes=[
            *scalars,
            pltpu.VMEM((n1, 128), bf16),
            pltpu.VMEM((n1, 1), f32),
            pltpu.VMEM((n1, D), bf16),
            pltpu.VMEM((nh, D), bf16),
            pltpu.VMEM((n1, D), bf16),
            pltpu.VMEM((n1, D), bf16),
            pltpu.VMEM((nh, D), bf16),
            pltpu.VMEM((D, D), bf16),
            pltpu.SemaphoreType.DMA((6,)),
        ],
        compiler_params=pltpu.CompilerParams(vmem_limit_bytes=VMEM_LIMIT),
        name="first",
    )(
        off_chip(logit_scale), on_chip(everyone), on_chip(table), on_chip(padded),
        *map(off_chip, (qkv_weight, out_weight, conv_weight)),
    )
    other = own
    if geo.sides == 2:
        other = lax.ppermute(own, "ha", [(n, n ^ 1) for n in range(down)])

    n0 = geo.r0n * geo.c0n * AREA
    ring = qc + 2
    whole = qr * ring * AREA
    strips = ring * STRIP * (3 - geo.sides)
    window = pltpu.VMEM((n0, D), bf16)
    wq1, wo1, wc = map(on_chip, (wq1, wo1, wc))
    limit = pltpu.CompilerParams(vmem_limit_bytes=VMEM_LIMIT)
    scale, everyone = off_chip(logit_scale), on_chip(everyone)
    state = pl.pallas_call(
        functools.partial(own_keys_body, geo),
        out_shape=(window,) * 3,
        in_specs=[vmem, vmem],
        out_specs=(vmem,) * 3,
        compiler_params=limit,
        name="own_keys",
    )(on_chip(own), wq1)
    pieces = pltpu.VMEM((whole + strips, D), bf16)
    edge, queries, att = pl.pallas_call(
        functools.partial(rows_body, geo),
        out_shape=(pltpu.VMEM((ring * TILE, D), bf16), pieces, pieces) + (window,) * 3,
        in_specs=[hbm] + [vmem] * 7,
        out_specs=(vmem,) * 6,
        input_output_aliases={5: 3, 6: 4, 7: 5},
        scratch_shapes=[*scalars, pieces, pltpu.SemaphoreType.DMA((2,))],
        compiler_params=limit,
        name="rows",
    )(scale, everyone, on_chip(other), wq1, wo1, *map(on_chip, state))[:3]
    received = edge
    if geo.sides == 2:
        received = lax.ppermute(edge, "ha", [(n, n ^ 1) for n in range(down)])
    middle, outer = pl.pallas_call(
        functools.partial(finish_body, geo),
        out_shape=(
            pltpu.VMEM((qr * TILE, ring * TILE, D), f32),
            pltpu.VMEM((ring * TILE * (3 - geo.sides), D), bf16),
        ),
        in_specs=[vmem] * 3,
        out_specs=(vmem,) * 2,
        compiler_params=limit,
        name="finish",
    )(on_chip(queries), on_chip(att), wo1)
    return pl.pallas_call(
        functools.partial(conv_body, geo),
        out_shape=jax.ShapeDtypeStruct((qr * TILE, qc * TILE, cout), bf16),
        in_specs=[vmem] * 4,
        out_specs=vmem,
        scratch_shapes=[pltpu.VMEM((2, ring * TILE, D), f32)],
        compiler_params=limit,
        name="conv",
    )(*map(on_chip, (middle, outer, received)), wc)


def solution(mesh):
    in_specs = (
        P(("parts", "ha", "wa"), None),
        P(("parts", "ha"), "wa", None),
        P(),
        P(),
        P(),
        P(),
        P(),
    )
    out_specs = P(("parts", "ha"), "wa", None)
    return jax.shard_map(local, mesh=mesh, in_specs=in_specs, out_specs=out_specs, check_vma=False)
```
